512 devices in a mesh: dp: 16 (over y, core), ctx: 32 (over z, x).
Axes of the slice: x: 4, y: 8, z: 8, core: 2. Of those that a mesh axis runs over, the one named last changes fastest.
Arguments:
- delta_query_rows: bfloat16 [16, 4096, 16, 128], P('dp', 'ctx'), may hold values from -6 to 6
- delta_key_rows: bfloat16 [16, 4096, 16, 128], P('dp', 'ctx'), may hold values from -6 to 6
- delta_value_rows: bfloat16 [16, 4096, 16, 128], P('dp', 'ctx'), may hold values from -6 to 6
- delta_write_strength: float32 [16, 4096, 16], P('dp', 'ctx'), may hold values from 0.2 to 1
- token_gate_scale: float32 [16, 4096, 16], P('dp', 'ctx'), may hold values from 0.5 to 2
- channel_decay_rate: float32 [16, 128], replicated, may hold values from 0.00390625 to 0.0625
- sudden_loss_mask: int32 [16, 4096], P('dp', 'ctx'), may hold values 0 or 1
- document_numbers: int32 [16, 4096], P('dp'), may hold values from 0 to 63, never falling along the last dimension, each value on 1 to 128 neighbouring positions
- delta_norm_gain: float32 [128], replicated, may hold values from 0.5 to 1.5
- delta_output_cotangent: bfloat16 [16, 4096, 16, 128], P('dp', 'ctx'), may hold values from -6 to 6
- latent_query_rows: bfloat16 [16, 4096, 16, 128], P('dp', 'ctx'), may hold values from -90 to 90
- compressed_latents: bfloat16 [16, 4096, 512], P('dp', 'ctx'), may hold values from -90 to 90
- query_to_latent_map: bfloat16 [16, 128, 512], P(None, 'ctx'), may hold values from -0.5 to 0.5
- latent_to_value_map: bfloat16 [16, 512, 128], P(None, 'ctx'), may hold values from -0.25 to 0.25
Outputs:
- kda_output: bfloat16 [16, 4096, 16, 128], P('dp', 'ctx')
- mla_output: bfloat16 [16, 4096, 16, 128], P('dp', 'ctx')
- gain_grad: float32 [128], replicated
The draws below stay inside these ranges and needn't reach their ends.
Inputs may be any that keep to these rules, and one draw needn't show every extreme that they name: `document_numbers`: each row's document numbers never fall; every document has 1 to 128 tokens, and some document has exactly 128.
All inputs are finite; a program needn't handle non-finite values. No bound on the sum of `sudden_loss_mask` on one device may be relied on, other than what follows from the above.
Results may differ from the reference program's by a relative error of at most 0.0065.
The reference program's roundings to bfloat16 on the way (of `lifted`, `probs` and `latent_mix`) count: a program that leaves them out, or rounds other values in their place, can miss the bound.
Values may be sent and summed in bfloat16 or wider, within the bound.
No kernel may reach another device: no remote copies, remote signals or barrier semaphores. Data moves between devices by JAX's collectives and lax.ppermute only.
A program may use at most 128 MiB of HBM per device.

```python
import math
import jax
import jax.numpy as jnp
import numpy as np
from jax import lax

HALF = 64
DOCBLK = 2
HK = 16
DK = 128
DV = 128
HM = 16
DN = 128
DL = 512
DVM = 128
MAXDOC = 128
PACKED_SEQUENCES = 16
SEQUENCE_TOKENS = 4096
N_CTX = 32


def draw_latent_query_rows(key, part):
    base = jax.random.normal(key, (PACKED_SEQUENCES, SEQUENCE_TOKENS, HM, DN), jnp.float32)
    return jnp.clip(base, -90.0, 90.0).astype(jnp.bfloat16)


def draw_compressed_latents(key, part):
    base = jax.random.normal(key, (PACKED_SEQUENCES, SEQUENCE_TOKENS, DL), jnp.float32)
    return jnp.clip(base, -90.0, 90.0).astype(jnp.bfloat16)


def touch_ends(drawn, key, smallest, largest):
    index_at = [jax.random.randint(jax.random.fold_in(key, axis), (), 0, length) for axis, length in enumerate(drawn.shape)]
    widest = drawn.shape.index(max(drawn.shape))
    beside = index_at[:widest] + [(index_at[widest] + 1) % drawn.shape[widest]] + index_at[widest + 1:]
    return drawn.at[tuple(index_at)].set(smallest).at[tuple(beside)].set(largest)


def shard_levels(rng, extent, pieces, low, largest):
    gain, own = 1.0, jax.random.fold_in(rng, 6)
    for position, parts in pieces:
        heights = jnp.exp(jax.random.uniform(jax.random.fold_in(own, position), (parts,), jnp.float32, low / len(pieces), largest / len(pieces)))
        gain = gain * jnp.repeat(heights, extent[position] // parts).reshape([-1 if axis == position else 1 for axis in range(len(extent))])
    return gain


def split_up(amount, total, bound, skew):
    weights = [(1 << 20) // math.isqrt(rank ** skew) + 1 for rank in range(2, amount + 1)]
    spare, holding = total - bound - (amount - 1), [1] * (amount - 1)
    while spare > 0:
        free = [i for i in range(amount - 1) if holding[i] < bound]
        mass, left = sum([weights[i] for i in free]), spare
        for i in free:
            addition = min(bound - holding[i], max(1, left * weights[i] // mass), spare)
            holding[i] = holding[i] + addition
            spare = spare - addition
    return np.array([bound] + holding)


def ragged_sizes(key, number_of, total, limit, slope):
    if number_of == 2:
        one = jax.random.randint(key, (), max(1, total - limit), min(limit, total - 1) + 1)
        return jnp.stack([one, total - one])
    lengths = jnp.asarray(split_up(number_of, total, limit, slope), jnp.int32)
    couples = (number_of - 1) // 2
    donor, sink = lengths[1:1 + 2 * couples:2], lengths[2:2 + 2 * couples:2]
    slack = jnp.minimum(donor - 1, limit - sink)
    shifted = jax.random.randint(jax.random.fold_in(key, 1), (couples,), 0, 1 << 20) % (slack + 1)
    lengths = lengths.at[1:1 + 2 * couples:2].set(donor - shifted).at[2:2 + 2 * couples:2].set(sink + shifted)
    return lengths[jax.random.permutation(jax.random.fold_in(key, 2), number_of)]


def normal_values(rng, extent, width, reach, cuts=(), kind=jnp.bfloat16):
    factor_of = shard_levels(rng, extent, cuts, -0.22, 0.18) if cuts else 1.0
    entries = jax.random.normal(rng, extent, jnp.float32) * width * factor_of
    return jnp.minimum(jnp.maximum(entries, -reach), reach).astype(kind)


def setup_inputs(seed: int = 0) -> dict:
    key_of = jax.random.split(jax.random.key(seed), 15)
    return {
        "delta_query_rows": normal_values(key_of[0], (PACKED_SEQUENCES, SEQUENCE_TOKENS, HK, DK), 1.0, 6.0, ((0, 16), (1, 32))),
        "delta_key_rows": normal_values(key_of[1], (PACKED_SEQUENCES, SEQUENCE_TOKENS, HK, DK), 1.0, 6.0, ((0, 16), (1, 32))),
        "delta_value_rows": normal_values(key_of[2], (PACKED_SEQUENCES, SEQUENCE_TOKENS, HK, DV), 1.0, 6.0, ((0, 16), (1, 32))),
        "delta_write_strength": jnp.clip(0.2 + 0.8 * jax.random.uniform(key_of[3], (PACKED_SEQUENCES, SEQUENCE_TOKENS, HK), jnp.float32) ** shard_levels(key_of[3], (PACKED_SEQUENCES, SEQUENCE_TOKENS, HK), ((0, 16), (1, 32)), -0.2, 0.2), 0.2, 1.0),
        "token_gate_scale": jnp.clip(0.5 + 1.5 * jax.random.uniform(key_of[4], (PACKED_SEQUENCES, SEQUENCE_TOKENS, HK), jnp.float32) ** shard_levels(key_of[4], (PACKED_SEQUENCES, SEQUENCE_TOKENS, HK), ((0, 16), (1, 32)), -0.2, 0.2), 0.5, 2.0),
        "channel_decay_rate": jnp.clip(jnp.exp(jax.random.uniform(key_of[5], (HK, DK), jnp.float32, math.log(0.00390625), math.log(0.0625))), 0.00390625, 0.0625),
        "sudden_loss_mask": touch_ends((jax.random.randint(key_of[6], (PACKED_SEQUENCES, SEQUENCE_TOKENS), 0, 32) < 1).astype(jnp.int32), jax.random.fold_in(key_of[6], 1), 0, 1),
        "document_numbers": jax.vmap(lambda own: jnp.searchsorted(jnp.cumsum(ragged_sizes(own, SEQUENCE_TOKENS // HALF, SEQUENCE_TOKENS, MAXDOC, 1)), jnp.arange(SEQUENCE_TOKENS), side="right"))(jax.random.split(key_of[7], PACKED_SEQUENCES)).reshape((PACKED_SEQUENCES, SEQUENCE_TOKENS)).astype(jnp.int32),
        "delta_norm_gain": jnp.clip(1.0 + 0.1 * jax.random.normal(key_of[8], (DV,), jnp.float32), 0.5, 1.5),
        "delta_output_cotangent": normal_values(key_of[9], (PACKED_SEQUENCES, SEQUENCE_TOKENS, HK, DV), 1.0, 6.0, ((0, 16), (1, 32))),
        "latent_query_rows": draw_latent_query_rows(jax.random.fold_in(key_of[14], 71), 0),
        "compressed_latents": draw_compressed_latents(jax.random.fold_in(key_of[14], 71), 0),
        "query_to_latent_map": normal_values(key_of[12], (HM, DN, DL), DN ** -0.5, 0.5, ((1, 32),)),
        "latent_to_value_map": normal_values(key_of[13], (HM, DL, DVM), DL ** -0.5, 0.25, ((1, 32),)),
    }


exact_mode = lax.Precision.HIGHEST

def into_natural_order(tensor):
    shape = tensor.shape
    blocks = tensor.reshape((shape[0], N_CTX, 2, HALF) + shape[2:])
    lower_half = blocks[:, :, 0]
    upper_half = jnp.flip(blocks[:, :, 1], axis=1)
    return jnp.concatenate([lower_half, upper_half], axis=1).reshape(shape)

def to_stored(tensor):
    shape = tensor.shape
    blocks = tensor.reshape((shape[0], 2, N_CTX, HALF) + shape[2:])
    lower_half = blocks[:, 0]
    upper_half = jnp.flip(blocks[:, 1], axis=1)
    return jnp.stack([lower_half, upper_half], axis=2).reshape(shape)

def unit_norm(tensor):
    widened = tensor.astype(jnp.float32)
    return widened * lax.rsqrt(lax.optimization_barrier(jnp.sum(widened * widened, axis=-1, keepdims=True)) + 1e-06)

def kda_block(state, inputs):
    queries, keyset, values, writes, log_decay_values, docs, before = inputs
    size = docs.shape[0]
    places = jnp.arange(size, dtype=jnp.int32)
    same_doc = docs[:, None] == docs[None, :]
    within = (same_doc & (places[:, None] >= places[None, :])).astype(jnp.float32)
    earlier = (same_doc & (places[:, None] > places[None, :])).astype(jnp.float32)
    cumlog = jnp.einsum('ts,shc->thc', within, log_decay_values, precision=exact_mode)
    key_decayed = keyset * jnp.exp(cumlog)
    key_grown = keyset * jnp.exp(-cumlog)
    query_decayed = queries * jnp.exp(cumlog)
    carried = (docs == before).astype(jnp.float32)
    pairwise = jnp.einsum('thc,shc->hts', key_decayed, key_grown, precision=exact_mode)
    triangle = pairwise * jnp.transpose(writes)[:, :, None] * earlier[None]
    projected = jnp.einsum('thc,hcv->thv', key_decayed, state, precision=exact_mode)
    targets = writes[:, :, None] * (values - carried[:, None, None] * projected)
    identity_mat = jnp.eye(size, dtype=jnp.float32)
    updates = jax.scipy.linalg.solve_triangular(identity_mat[None] + triangle, jnp.transpose(targets, (1, 0, 2)), lower=True, unit_diagonal=True)
    weights_att = jnp.einsum('thc,shc->hts', query_decayed, key_grown, precision=exact_mode) * within[None]
    output = carried[:, None, None] * jnp.einsum('thc,hcv->thv', query_decayed, state, precision=exact_mode)
    output = output + jnp.einsum('hts,hsv->thv', weights_att, updates, precision=exact_mode)
    closing = jnp.exp(cumlog[size - 1])
    tailing = (docs == docs[size - 1]).astype(jnp.float32)
    leaving = key_grown * closing[None] * tailing[:, None, None]
    new_state = carried[size - 1] * closing[:, :, None] * state
    new_state = new_state + jnp.einsum('shc,hsv->hcv', leaving, updates, precision=exact_mode)
    return (new_state, output)

def kda_sequence(queries, keyset, values, writes, log_decay_values, docs):
    count = docs.shape[0] // HALF

    def blocked(tensor):
        return tensor.reshape((count, HALF) + tensor.shape[1:])
    endings = docs.reshape(count, HALF)[:, HALF - 1]
    before = jnp.concatenate([jnp.full((1,), -1, jnp.int32), endings[:-1]])
    start_state = jnp.zeros((HK, DK, DV), jnp.float32)
    final_state, outputs = lax.scan(kda_block, start_state, (blocked(queries), blocked(keyset), blocked(values), blocked(writes), blocked(log_decay_values), blocked(docs), before))
    return outputs.reshape(docs.shape[0], HK, DV)

def mla_sequence(queries, latents, docs, query_to_latent_map, latent_to_value_map):
    lifted = jnp.einsum('thn,hnl->thl', queries.astype(jnp.float32), query_to_latent_map.astype(jnp.float32)).astype(jnp.bfloat16)
    margin = DOCBLK * HALF
    padded = jnp.concatenate([jnp.zeros((margin, DL), jnp.bfloat16), latents], axis=0)
    padded_docs = jnp.concatenate([jnp.full((margin,), -1, jnp.int32), docs])
    count = docs.shape[0] // HALF
    scale = 1.0 / math.sqrt(DN)

    def one_block(block):
        start = (block * HALF).astype(jnp.int32)
        block_query = lax.dynamic_slice_in_dim(lifted, start, HALF, 0)
        key_rows = lax.dynamic_slice_in_dim(padded, start, margin + HALF, 0)
        key_docs = lax.dynamic_slice_in_dim(padded_docs, start, margin + HALF, 0)
        query_docs = lax.dynamic_slice_in_dim(docs, start, HALF, 0)
        key_pos = start - margin + jnp.arange(margin + HALF, dtype=jnp.int32)
        query_pos = start + jnp.arange(HALF, dtype=jnp.int32)
        logits = jnp.einsum('thl,kl->htk', block_query.astype(jnp.float32), key_rows.astype(jnp.float32)) * scale
        allowed = (query_docs[None, :, None] == key_docs[None, None, :]) & (key_pos[None, None, :] <= query_pos[None, :, None])
        logits = jnp.where(allowed, logits, -jnp.inf)
        peak = lax.optimization_barrier(jnp.max(logits, axis=-1, keepdims=True))
        expo = jnp.exp(logits - peak)
        probs = (expo / lax.optimization_barrier(jnp.sum(expo, axis=-1, keepdims=True))).astype(jnp.bfloat16)
        latent_mix = jnp.einsum('htk,kl->thl', probs.astype(jnp.float32), key_rows.astype(jnp.float32)).astype(jnp.bfloat16)
        return jnp.einsum('thl,hlv->thv', latent_mix.astype(jnp.float32), latent_to_value_map.astype(jnp.float32)).astype(jnp.bfloat16)
    outputs = lax.map(one_block, jnp.arange(count, dtype=jnp.int32))
    return outputs.reshape(docs.shape[0], HM, DVM)

def reference(delta_query_rows, delta_key_rows, delta_value_rows, delta_write_strength, token_gate_scale, channel_decay_rate, sudden_loss_mask, document_numbers, delta_norm_gain, delta_output_cotangent, latent_query_rows, compressed_latents, query_to_latent_map, latent_to_value_map):
    queries = unit_norm(into_natural_order(delta_query_rows))
    keyset = unit_norm(into_natural_order(delta_key_rows))
    values = into_natural_order(delta_value_rows).astype(jnp.float32)
    writes = into_natural_order(delta_write_strength)
    scale_factors = into_natural_order(token_gate_scale)
    sudden_losses = into_natural_order(sudden_loss_mask).astype(jnp.float32)
    log_decay_values = -channel_decay_rate[None, None] * scale_factors[..., None] + sudden_losses[:, :, None, None] * math.log(0.6)
    kda_raw = lax.map(lambda members: kda_sequence(*members), (queries, keyset, values, writes, log_decay_values, document_numbers))
    meansq = lax.optimization_barrier(jnp.mean(kda_raw * kda_raw, axis=-1, keepdims=True))
    normed = kda_raw * lax.rsqrt(meansq + 1e-06)
    kda_output = to_stored((normed * delta_norm_gain).astype(jnp.bfloat16))
    gain_grad = lax.optimization_barrier(jnp.sum(normed * into_natural_order(delta_output_cotangent).astype(jnp.float32), axis=(0, 1, 2))) / math.sqrt(PACKED_SEQUENCES * SEQUENCE_TOKENS * HK)
    mla_natural = lax.map(lambda members: mla_sequence(members[0], members[1], members[2], query_to_latent_map, latent_to_value_map), (into_natural_order(latent_query_rows), into_natural_order(compressed_latents), document_numbers))
    return (kda_output, to_stored(mla_natural), gain_grad)
```

```python
import functools
import math

import jax
import jax.numpy as jnp
from jax import lax
from jax.experimental import pallas as pl
from jax.experimental.pallas import tpu as pltpu
from jax.sharding import PartitionSpec as P

DN = 128
XS = 4
HALF = 64
F32 = jnp.float32
BF = jnp.bfloat16
LOSS = math.log(0.6)


def mm(a, b):
    return lax.dot_general(a, b, (((1,), (0,)), ((), ())), preferred_element_type=F32)


def mm_nt(a, b):
    return lax.dot_general(a, b, (((1,), (1,)), ((), ())), preferred_element_type=F32)


def mm_tn(a, b):
    return lax.dot_general(a, b, (((0,), (0,)), ((), ())), preferred_element_type=F32)


def iota2(shape, dim):
    return lax.broadcasted_iota(jnp.int32, shape, dim)


def docs_row(docs_ref, block):
    row = docs_ref[pl.ds(block // 2, 1), :].astype(F32)
    odd = jnp.full((1, HALF), block % 2, jnp.int32)
    return jnp.where(odd == 1, row[:, HALF:], row[:, :HALF])


def as_column(row):
    size = row.shape[1]
    eye = iota2((size, size), 0) == iota2((size, size), 1)
    return jnp.sum(jnp.where(eye, jnp.broadcast_to(row, (size, size)), 0.0), axis=1, keepdims=True)


def kda_pairs_kernel(
    place_ref, q_ref, k_ref, v_ref, w_ref, scale_ref, rate_ref, mask_ref, docs_ref,
    lmat, att, rhs, leaving, closing, carried_q,
    qn, kn, vn, acol, wcol, bcol, ccol, tcol, incl, excl,
):
    heads = rate_ref.shape[0]
    place = place_ref[0]
    ranks = docs_ref.shape[0]
    rows = HALF * heads

    def widen(c, _):
        at = pl.ds(pl.multiple_of(c * 256, 256), 256)
        for source, target in ((q_ref, qn), (k_ref, kn)):
            x = source[at, :].astype(F32)
            target[at, :] = x * lax.rsqrt(jnp.sum(x * x, axis=1, keepdims=True) + 1e-06)
        vn[at, :] = v_ref[at, :].astype(F32)
        return 0

    lax.fori_loop(0, 2 * rows // 256, widen, 0)
    ti, si = iota2((HALF, HALF), 0), iota2((HALF, HALF), 1)
    for i in range(2):
        block = place if i == 0 else 2 * ranks - 1 - place
        drow = docs_row(docs_ref, block)
        prior = docs_row(docs_ref, jnp.maximum(block - 1, 0))[:, HALF - 1 :]
        prior = jnp.where(jnp.full((1, 1), block, jnp.int32) > 0, prior, -1.0)
        dcol = as_column(drow)
        same = dcol == drow
        within = jnp.where(same & (ti >= si), 1.0, 0.0)
        incl[i] = within
        excl[i] = jnp.where(same & (ti > si), 1.0, 0.0)
        gates = lax.dot_general(
            within, scale_ref[i * HALF : (i + 1) * HALF, :], (((1,), (0,)), ((), ())),
            precision=lax.Precision.HIGHEST, preferred_element_type=F32,
        )
        lost = mask_ref[:, i * HALF : (i + 1) * HALF].astype(F32)
        bcol[i] = jnp.broadcast_to(jnp.sum(within * lost, axis=1, keepdims=True) * LOSS, (HALF, DN))
        ccol[i] = jnp.broadcast_to(jnp.where(dcol == prior, 1.0, 0.0), (HALF, DN))
        tcol[i] = jnp.broadcast_to(jnp.where(dcol == drow[:, HALF - 1 :], 1.0, 0.0), (HALF, DN))
        writes = w_ref[i * HALF : (i + 1) * HALF, :]
        for h in range(heads):
            acol[i * heads + h] = jnp.broadcast_to(gates[:, h : h + 1], (HALF, DN))
            wcol[i * heads + h] = jnp.broadcast_to(writes[:, h : h + 1], (HALF, DN))

    def pairs(g, _):
        for u in range(4):
            p = g * 4 + u
            i = p // heads
            h = p % heads
            at = pl.ds(i * rows + h, HALF, stride=heads)
            q, k, v = qn[at, :], kn[at, :], vn[at, :]
            w = wcol[p]
            carried = ccol[i]
            cumlog = bcol[i] - acol[p] * rate_ref[pl.ds(h, 1), :]
            grow = jnp.exp(cumlog)
            kd, qd = k * grow, q * grow
            kg = k * jnp.exp(-cumlog)
            both = jnp.concatenate([kd, qd], axis=0)
            both_hi, kg_hi = both.astype(BF), kg.astype(BF)
            both_lo = (both - both_hi.astype(F32)).astype(BF)
            kg_lo = (kg - kg_hi.astype(F32)).astype(BF)
            inner = mm_nt(both_hi, kg_hi) + mm_nt(both_hi, kg_lo) + mm_nt(both_lo, kg_hi)
            lmat[p] = inner[:HALF] * w[:, :HALF] * excl[i]
            att[p] = (inner[HALF:] * incl[i]).astype(BF)
            rhs[p, :, :DN] = (w * v).astype(BF)
            rhs[p, :, DN:] = (w * carried * kd).astype(BF)
            carried_q[p] = (carried * qd).astype(BF)
            last = grow[HALF - 1 :, :]
            leaving[p] = (kg * last * tcol[i]).astype(BF)
            closing[p] = jnp.broadcast_to(carried[HALF - 1 :, :] * last, (8, DN))
        return 0

    lax.fori_loop(0, 2 * heads // 4, pairs, 0)


def kda_pairs(place, q, k, v, w, scale, rate, mask, docs):
    heads = rate.shape[0]
    n = 2 * heads
    rows = q.shape[0]
    vm = lambda *s: pltpu.VMEM(s, F32)
    spec = pl.BlockSpec(memory_space=pltpu.VMEM)
    shapes = (
        jax.ShapeDtypeStruct((n, HALF, HALF), F32),
        jax.ShapeDtypeStruct((n, HALF, HALF), BF),
        jax.ShapeDtypeStruct((n, HALF, 2 * DN), BF),
        jax.ShapeDtypeStruct((n, HALF, DN), BF),
        jax.ShapeDtypeStruct((n, 8, DN), F32),
        jax.ShapeDtypeStruct((n, HALF, DN), BF),
    )
    return pl.pallas_call(
        kda_pairs_kernel,
        name="kda_pairs",
        out_shape=shapes,
        in_specs=[pl.BlockSpec(memory_space=pltpu.SMEM)] + [spec] * 8,
        out_specs=(spec,) * 6,
        scratch_shapes=[
            vm(rows, DN), vm(rows, DN), vm(rows, DN),
            vm(n, HALF, DN), vm(n, HALF, DN),
            vm(2, HALF, DN), vm(2, HALF, DN), vm(2, HALF, DN),
            vm(2, HALF, HALF), vm(2, HALF, HALF),
        ],
        compiler_params=pltpu.CompilerParams(vmem_limit_bytes=32 << 20),
        cost_estimate=pl.CostEstimate(flops=300_000_000, bytes_accessed=12_000_000, transcendentals=600_000),
    )(place, q, k, v, w, scale, rate, mask, docs)


def kda_invert_kernel(lmat, xmat):
    heads = lmat.shape[0] // 2
    ti, si = iota2((HALF, HALF), 0), iota2((HALF, HALF), 1)

    def base(g, _):
        for u in range(2):
            p = g * 2 + u
            lower = lmat[p]
            for b in range(HALF // 16):
                x = jnp.where(iota2((16, HALF), 0) + 16 * b == iota2((16, HALF), 1), 1.0, 0.0)
                part = lower[16 * b : 16 * b + 16, :]
                for j in range(15):
                    x = x - part[:, 16 * b + j : 16 * b + j + 1] * x[j : j + 1, :]
                xmat[p, 16 * b : 16 * b + 16, :] = x
        return 0

    lax.fori_loop(0, heads, base, 0)

    def merge(width, g, _):
        tb, sb = ti // width, si // width
        cross = ((tb % 2) == 1) & (sb == tb - 1)
        for u in range(8):
            p = g * 8 + u
            x = xmat[p]
            xb = x.astype(BF)
            y = mm(jnp.where(cross, lmat[p], 0.0).astype(BF), xb)
            xmat[p] = x - mm(xb, y.astype(BF))
        return 0

    lax.fori_loop(0, heads // 4, functools.partial(merge, 16), 0)
    lax.fori_loop(0, heads // 4, functools.partial(merge, 32), 0)


def kda_invert(lmat):
    spec = pl.BlockSpec(memory_space=pltpu.VMEM)
    return pl.pallas_call(
        kda_invert_kernel,
        name="kda_invert",
        out_shape=jax.ShapeDtypeStruct(lmat.shape, F32),
        in_specs=[spec],
        out_specs=spec,
        compiler_params=pltpu.CompilerParams(vmem_limit_bytes=16 << 20),
        cost_estimate=pl.CostEstimate(flops=300_000_000, bytes_accessed=12_000_000, transcendentals=0),
    )(lmat)


def kda_leave_kernel(xmat, rhs, leaving, closing, lat_ref, offs_first, offs_second, tmap, upd):
    heads = xmat.shape[0] // 2
    base_row = heads * DN
    for lb in range(4):
        part = lat_ref[:, lb * DN : (lb + 1) * DN]
        low = base_row + lb * HALF
        offs_first[low : low + HALF, :] = part[:HALF]
        offs_second[low : low + HALF, :] = part[:HALF]
        offs_second[low + 4 * HALF : low + 5 * HALF, :] = part[HALF:]

    def solve(g, _):
        for u in range(8):
            p = g * 8 + u
            upd[p] = mm(xmat[p].astype(BF), rhs[p]).astype(BF)
        return 0

    lax.fori_loop(0, heads // 4, solve, 0)

    eye = iota2((DN, DN), 0) == iota2((DN, DN), 1)
    for i, target in ((0, offs_first), (1, offs_second)):

        def leave(g, _, i=i, target=target):
            for u in range(4):
                h = g * 4 + u
                p = i * heads + h
                made = mm_tn(leaving[p], upd[p])
                target[pl.ds(pl.multiple_of(h * DN, DN), DN), :] = made[:, :DN].astype(BF)
                keep = jnp.where(eye, jnp.broadcast_to(closing[p][:1, :], (DN, DN)), 0.0)
                tmap[p] = (keep - made[:, DN:]).astype(BF)
            return 0

        lax.fori_loop(0, heads // 4, leave, 0)


def kda_leave(xmat, rhs, leaving, closing, latents):
    n = xmat.shape[0]
    spec = pl.BlockSpec(memory_space=pltpu.VMEM)
    shapes = (
        jax.ShapeDtypeStruct((n // 2 * DN + 4 * HALF, DN), BF),
        jax.ShapeDtypeStruct((n // 2 * DN + 8 * HALF, DN), BF),
        jax.ShapeDtypeStruct((n, DN, DN), BF),
        jax.ShapeDtypeStruct((n, HALF, 2 * DN), BF),
    )
    return pl.pallas_call(
        kda_leave_kernel,
        name="kda_leave",
        out_shape=shapes,
        in_specs=[spec] * 5,
        out_specs=(spec,) * 4,
        compiler_params=pltpu.CompilerParams(vmem_limit_bytes=24 << 20),
        cost_estimate=pl.CostEstimate(flops=300_000_000, bytes_accessed=8_000_000, transcendentals=0),
    )(xmat, rhs, leaving, closing, latents)


def kda_local_kernel(att, upd, carried_q, local, squery):
    n = att.shape[0]

    def body(g, _):
        for u in range(8):
            p = g * 8 + u
            made = mm(att[p], upd[p])
            local[p] = made[:, :DN]
            squery[p] = (carried_q[p].astype(F32) - made[:, DN:]).astype(BF)
        return 0

    lax.fori_loop(0, n // 8, body, 0)


def kda_local(att, upd, carried_q):
    n = att.shape[0]
    spec = pl.BlockSpec(memory_space=pltpu.VMEM)
    return pl.pallas_call(
        kda_local_kernel,
        name="kda_local",
        out_shape=(jax.ShapeDtypeStruct((n, HALF, DN), F32), jax.ShapeDtypeStruct((n, HALF, DN), BF)),
        in_specs=[spec] * 3,
        out_specs=(spec,) * 2,
        cost_estimate=pl.CostEstimate(flops=70_000_000, bytes_accessed=4_000_000, transcendentals=0),
    )(att, upd, carried_q)


def kda_carry_kernel(place_ref, tmap, offs_first, offs_second, in_first, in_second, out_first, out_second, *, ranks):
    heads = tmap.shape[0] // 2
    end = jnp.full((DN, DN), place_ref[0], jnp.int32) == ranks - 1
    low = heads * DN
    out_first[low:, :] = in_first[low:, :]
    out_second[low:, :] = in_second[low + 4 * HALF :, :]

    def body(g, _):
        for u in range(4):
            h = g * 4 + u
            at = pl.ds(pl.multiple_of(h * DN, DN), DN)
            own = offs_first[at, :].astype(F32)
            out_first[at, :] = (own + mm(tmap[h], in_first[at, :])).astype(BF)
            upper = jnp.where(end, own, in_second[at, :].astype(F32)).astype(BF)
            out_second[at, :] = (
                offs_second[at, :].astype(F32) + mm(tmap[heads + h], upper)
            ).astype(BF)
        return 0

    lax.fori_loop(0, heads // 4, body, 0)


def kda_carry(place, tmap, offs_first, offs_second, in_first, in_second, ranks):
    spec = pl.BlockSpec(memory_space=pltpu.VMEM)
    shape = jax.ShapeDtypeStruct(offs_first.shape, BF)
    return pl.pallas_call(
        functools.partial(kda_carry_kernel, ranks=ranks),
        name="kda_carry",
        out_shape=(shape, shape),
        in_specs=[pl.BlockSpec(memory_space=pltpu.SMEM)] + [spec] * 5,
        out_specs=(spec, spec),
        cost_estimate=pl.CostEstimate(flops=130_000_000, bytes_accessed=5_000_000, transcendentals=0),
    )(place, tmap, offs_first, offs_second, in_first, in_second)


def kda_close_kernel(place_ref, local, squery, own_first, in_first, in_second, gain, cot_ref, out_ref, grad_ref, cot, outs, *, ranks):
    heads = local.shape[0] // 2
    rows = HALF * heads
    end = jnp.full((DN, DN), place_ref[0], jnp.int32) == ranks - 1

    def widen(c, _):
        at = pl.ds(pl.multiple_of(c * 256, 256), 256)
        cot[at, :] = cot_ref[at, :].astype(F32)
        return 0

    lax.fori_loop(0, 2 * rows // 256, widen, 0)

    def body(g, grad):
        for u in range(4):
            h = g * 4 + u
            state_at = pl.ds(pl.multiple_of(h * DN, DN), DN)
            upper = jnp.where(
                end, own_first[state_at, :].astype(F32), in_second[state_at, :].astype(F32)
            ).astype(BF)
            for i, state in ((0, in_first[state_at, :]), (1, upper)):
                p = i * heads + h
                raw = local[p] + mm(squery[p], state)
                normed = raw * lax.rsqrt(jnp.mean(raw * raw, axis=1, keepdims=True) + 1e-06)
                at = pl.ds(i * rows + h, HALF, stride=heads)
                outs[at, :] = normed * gain[...]
                terms = normed * cot[at, :]
                grad = grad + jnp.sum(terms.reshape(HALF // 8, 8, DN), axis=0)
        return grad

    grad = lax.fori_loop(0, heads // 4, body, jnp.zeros((8, DN), F32))
    grad_ref[...] = jnp.broadcast_to(jnp.sum(grad, axis=0, keepdims=True), grad_ref.shape)

    def narrow(c, _):
        at = pl.ds(pl.multiple_of(c * 256, 256), 256)
        out_ref[at, :] = outs[at, :].astype(BF)
        return 0

    lax.fori_loop(0, 2 * rows // 256, narrow, 0)


def kda_close(place, local, squery, own_first, in_first, in_second, gain, cot, ranks):
    spec = pl.BlockSpec(memory_space=pltpu.VMEM)
    rows = cot.shape[0]
    return pl.pallas_call(
        functools.partial(kda_close_kernel, ranks=ranks),
        name="kda_close",
        out_shape=(jax.ShapeDtypeStruct((rows, DN), BF), jax.ShapeDtypeStruct((ranks, DN), F32)),
        in_specs=[pl.BlockSpec(memory_space=pltpu.SMEM)] + [spec] * 7,
        out_specs=(spec, spec),
        scratch_shapes=[pltpu.VMEM((rows, DN), F32), pltpu.VMEM((rows, DN), F32)],
        compiler_params=pltpu.CompilerParams(vmem_limit_bytes=32 << 20),
        cost_estimate=pl.CostEstimate(flops=70_000_000, bytes_accessed=5_000_000, transcendentals=4096),
    )(place, local, squery, own_first, in_first, in_second, gain, cot)


def onehot(shape, source):
    return jnp.where(iota2(shape, 0) == source(iota2(shape, 1)), 1.0, 0.0).astype(BF)


def mla_kernel(
    spot_ref, q_ref, lat_ref, back_one, ahead_one, back_two, ahead_two, docs_ref, own_w, other_w, out_ref,
    qp, keys, keysp, mask, lifted, mixed, outs, *, xs,
):
    ranks = docs_ref.shape[0]
    place, core = spot_ref[0], spot_ref[1]
    heads = q_ref.shape[0] // (2 * HALF)
    here_z, here_x = place // xs, place % xs
    width = keys.shape[1]

    def piece(ref, at, i, slot):
        for lb in range(4):
            keys[i, slot * HALF : (slot + 1) * HALF, lb * DN : (lb + 1) * DN] = ref[
                at + lb * HALF : at + (lb + 1) * HALF, :
            ]

    keys[0, 3 * HALF :, :] = jnp.zeros((width - 3 * HALF, 4 * DN), BF)
    keys[1, 3 * HALF :, :] = jnp.zeros((width - 3 * HALF, 4 * DN), BF)
    low = heads * DN
    piece(back_two, low, 0, 0)
    piece(back_one, low, 0, 1)
    keys[0, 2 * HALF : 3 * HALF, :] = lat_ref[:HALF, :]
    keys[1, 2 * HALF : 3 * HALF, :] = lat_ref[HALF:, :]

    @pl.when(place < ranks - 2)
    def _():
        piece(ahead_two, low, 1, 0)

    @pl.when(place == ranks - 2)
    def _():
        piece(ahead_one, low, 1, 0)

    @pl.when(place == ranks - 1)
    def _():
        piece(back_one, low, 1, 0)
        keys[1, HALF : 2 * HALF, :] = lat_ref[:HALF, :]

    @pl.when(place < ranks - 1)
    def _():
        piece(ahead_one, low + 4 * HALF, 1, 1)

    def source_n(k):
        off = ((k // 4) % 2) * 4 + ((k // 8) % 2) * 2 + (k // 16) % 2
        z = lax.bitwise_xor(off, jnp.full(k.shape, here_z, jnp.int32))
        return (z * xs + (k // 32 + here_x) % xs) * 4 + k % 4

    def source_l(k):
        off = ((k // 16) % 2) * 4 + ((k // 32) % 2) * 2 + (k // 64) % 2
        z = lax.bitwise_xor(off, jnp.full(k.shape, here_z, jnp.int32))
        return (z * xs + (k // 128 + here_x) % xs) * 16 + k % 16

    pick = onehot((DN, DN), source_n)
    rows = 256

    def place_q(c, _):
        at = pl.ds(pl.multiple_of(c * rows, rows), rows)
        qp[at, :] = mm(q_ref[at, :], pick)
        return 0

    lax.fori_loop(0, q_ref.shape[0] // rows, place_q, 0)
    spread = onehot((4 * DN, 4 * DN), source_l)
    ti, si = iota2((HALF, HALF), 0), iota2((HALF, HALF), 1)
    for i in range(2):
        keysp[i] = mm(keys[i], spread).astype(BF)
        block = place if i == 0 else 2 * ranks - 1 - place
        drow = docs_row(docs_ref, block)
        dcol = as_column(drow)
        for back in range(3):
            source = block - back
            krow = docs_row(docs_ref, jnp.maximum(source, 0))
            krow = jnp.where(jnp.full((1, HALF), source, jnp.int32) >= 0, krow, -1.0)
            allowed = dcol == krow
            if back == 0:
                allowed = allowed & (ti >= si)
            fill = jnp.where(allowed, 0.0, -1e30)
            for r in range(4):
                mask[i, r * HALF : (r + 1) * HALF, (2 - back) * HALF : (3 - back) * HALF] = fill
        mask[i, :, 3 * HALF :] = jnp.full((4 * HALF, width - 3 * HALF), -1e30, F32)

    span = heads // 2
    for side, weights in ((0, own_w), (1, other_w)):
        first = span * core if side == 0 else span * (1 - core)

        def lift(g, _, weights=weights, first=first):
            for u in range(2):
                hl = g * 2 + u
                h = first + hl
                q = qp[pl.ds(h, 2 * HALF, stride=heads), :].astype(BF)
                for lb in range(4):
                    at = pl.ds(pl.multiple_of((hl * 4 + lb) * 16, 16), 16)
                    w = jnp.concatenate(
                        [weights[xr, e, at, :] for xr in range(4) for e in range(2)], axis=0
                    )
                    made = mm(q, w).astype(BF)
                    for i in range(2):
                        dst = pl.ds(pl.multiple_of(h * HALF, HALF), HALF)
                        lifted[i, dst, lb * DN : (lb + 1) * DN] = made[i * HALF : (i + 1) * HALF]
            return 0

        lax.fori_loop(0, span // 2, lift, 0)

    scale = 1.0 / math.sqrt(DN)

    def attend(g, _):
        i = g // (heads // 4)
        at = pl.ds(pl.multiple_of((g % (heads // 4)) * rows, rows), rows)
        logits = mm_nt(lifted[i, at, :], keys[i]) * scale + mask[i]
        peak = jnp.max(logits, axis=1, keepdims=True)
        expo = jnp.exp(logits - peak)
        probs = (expo / jnp.sum(expo, axis=1, keepdims=True)).astype(BF)
        mixed[i, at, :] = mm(probs, keysp[i]).astype(BF)
        return 0

    lax.fori_loop(0, heads // 2, attend, 0)

    for side, weights in ((0, own_w), (1, other_w)):
        first = span * core if side == 0 else span * (1 - core)

        def lower(g, _, weights=weights, first=first):
            for u in range(2):
                hl = g * 2 + u
                h = first + hl
                w = jnp.concatenate(
                    [
                        weights[xr, e, pl.ds(pl.multiple_of(512 + (zr * span + hl) * 16, 16), 16), :]
                        for xr in range(4) for e in range(2) for zr in range(4)
                    ],
                    axis=0,
                )
                src = pl.ds(pl.multiple_of(h * HALF, HALF), HALF)
                both = jnp.concatenate([mixed[0, src, :], mixed[1, src, :]], axis=0)
                outs[pl.ds(h, 2 * HALF, stride=heads), :] = mm(both, w)
            return 0

        lax.fori_loop(0, span // 2, lower, 0)

    def narrow(c, _):
        at = pl.ds(pl.multiple_of(c * rows, rows), rows)
        out_ref[at, :] = outs[at, :].astype(BF)
        return 0

    lax.fori_loop(0, q_ref.shape[0] // rows, narrow, 0)


def mla(spot, q, latents, back_one, ahead_one, back_two, ahead_two, docs, own_w, other_w, xs):
    spec = pl.BlockSpec(memory_space=pltpu.VMEM)
    rows = q.shape[0]
    return pl.pallas_call(
        functools.partial(mla_kernel, xs=xs),
        name="mla",
        out_shape=jax.ShapeDtypeStruct((rows, DN), BF),
        in_specs=[pl.BlockSpec(memory_space=pltpu.SMEM)] + [spec] * 9,
        out_specs=spec,
        scratch_shapes=[
            pltpu.VMEM((rows, DN), F32),
            pltpu.VMEM((2, 256, 4 * DN), BF),
            pltpu.VMEM((2, 256, 4 * DN), BF),
            pltpu.VMEM((2, 256, 256), F32),
            pltpu.VMEM((2, rows // 2, 4 * DN), BF),
            pltpu.VMEM((2, rows // 2, 4 * DN), BF),
            pltpu.VMEM((rows, DN), F32),
        ],
        compiler_params=pltpu.CompilerParams(vmem_limit_bytes=40 << 20),
        cost_estimate=pl.CostEstimate(flops=1_500_000_000, bytes_accessed=7_000_000, transcendentals=600_000),
    )(spot, q, latents, back_one, ahead_one, back_two, ahead_two, docs, own_w, other_w)


def from_behind(value, axis, steps):
    count = lax.axis_size(axis)
    leading, last = (max(0, -steps), min(count, count - steps))
    return lax.ppermute(value, axis, [(source, source + steps) for source in range(leading, last)])


def shards(
    delta_query_rows,
    delta_key_rows,
    delta_value_rows,
    delta_write_strength,
    token_gate_scale,
    channel_decay_rate,
    sudden_loss_mask,
    document_numbers,
    delta_norm_gain,
    delta_output_cotangent,
    latent_query_rows,
    compressed_latents,
    query_to_latent_map,
    latent_to_value_map,
):
    ranks = lax.axis_size("ctx")
    place = lax.axis_index("ctx")
    seqs = delta_query_rows.shape[0]
    rows = delta_query_rows.shape[1]
    heads = delta_query_rows.shape[2]
    value_width = delta_value_rows.shape[3]
    here = place.astype(jnp.int32).reshape(1)
    docs = document_numbers.reshape(ranks, rows)
    latents = compressed_latents[0]
    flat = lambda tensor: tensor.reshape(rows * heads, tensor.shape[3])

    groups = lax.axis_size("dp")
    member = lax.axis_index("dp")
    core = member % 2
    span = heads // 2
    keep_lift = lax.dynamic_slice_in_dim(query_to_latent_map, core * span, span, 0)
    keep_lower = lax.dynamic_slice_in_dim(latent_to_value_map, core * span, span, 0)
    lift_rows = keep_lift.reshape(span, 4, 4, DN).transpose(0, 2, 1, 3).reshape(span * 16, DN)
    held = jnp.concatenate([lift_rows, keep_lower.reshape(span * 16, DN)], axis=0)

    def across(value, step):
        return lax.ppermute(value, "ctx", [(i, i ^ step) for i in range(ranks)])

    held = jnp.stack([held, across(held, 4 * XS)])
    held = jnp.stack([held, across(held, 2 * XS)])
    lift_tiles = held[:, :, : span * 16].reshape(2, 2, span, 4, 4, DN)
    lift_tiles = lift_tiles.transpose(2, 3, 0, 1, 4, 5).reshape(span * 64, DN)
    held = jnp.concatenate([lift_tiles, held[:, :, span * 16 :].reshape(span * 64, DN)], axis=0)
    held = jnp.stack([held, across(held, XS)])

    lmat, att, rhs, leaving, closing, carried_q = kda_pairs(
        here,
        flat(delta_query_rows),
        flat(delta_key_rows),
        flat(delta_value_rows),
        delta_write_strength[0],
        token_gate_scale[0],
        channel_decay_rate,
        sudden_loss_mask,
        docs,
    )
    xmat = kda_invert(lmat)
    offs_first, offs_second, tmap, upd = kda_leave(xmat, rhs, leaving, closing, latents)
    near_first = from_behind(offs_first, "ctx", 1)
    near_second = from_behind(offs_second, "ctx", -1)
    columns = [held]
    for step in range(1, XS):
        pairs = [(i - i % XS + (i + step) % XS, i) for i in range(ranks)]
        columns.append(lax.ppermute(held, "ctx", pairs))
    own_w = jnp.stack(columns)
    other_w = lax.ppermute(own_w, "dp", [(i, i ^ 1) for i in range(groups)])

    local, squery = kda_local(att, upd, carried_q)
    out_first, out_second = kda_carry(
        here, tmap, offs_first, offs_second, near_first, near_second, ranks
    )
    far_first = from_behind(out_first, "ctx", 1)
    far_second = from_behind(out_second, "ctx", -1)
    normed_rows, partial_grad = kda_close(
        here,
        local,
        squery,
        out_first,
        far_first,
        far_second,
        delta_norm_gain.reshape(1, value_width),
        flat(delta_output_cotangent),
        ranks,
    )
    kda_output = normed_rows.reshape(seqs, rows, heads, value_width)
    along = jnp.sum(lax.all_to_all(partial_grad, "ctx", 0, 0, tiled=True), axis=0)
    spread = jnp.broadcast_to(along, (groups, value_width))
    total_grad = jnp.sum(lax.all_to_all(spread, "dp", 0, 0, tiled=True), axis=0)
    gain_grad = total_grad / math.sqrt(seqs * groups * rows * ranks * heads)

    spot = jnp.stack([place, core]).astype(jnp.int32)
    mla_rows = mla(
        spot,
        flat(latent_query_rows),
        latents,
        near_first,
        near_second,
        far_first,
        far_second,
        docs,
        own_w,
        other_w,
        XS,
    )
    mla_output = mla_rows.reshape(seqs, rows, heads, DN)
    return (kda_output, mla_output, gain_grad)


def solution(mesh):
    placed = (
        P("dp", "ctx", None, None),
        P("dp", "ctx", None, None),
        P("dp", "ctx", None, None),
        P("dp", "ctx", None),
        P("dp", "ctx", None),
        P(),
        P("dp", "ctx"),
        P("dp", None),
        P(),
        P("dp", "ctx", None, None),
        P("dp", "ctx", None, None),
        P("dp", "ctx", None),
        P(None, "ctx", None),
        P(None, "ctx", None),
    )
    return jax.shard_map(
        shards,
        mesh=mesh,
        in_specs=placed,
        out_specs=(P("dp", "ctx", None, None), P("dp", "ctx", None, None), P()),
        check_vma=False,
    )
```

```python
import functools
import math

import jax
import jax.numpy as jnp
from jax import lax
from jax.experimental import pallas as pl
from jax.experimental.pallas import tpu as pltpu
from jax.sharding import PartitionSpec as P

DN = 128
XS = 4
HALF = 64
F32 = jnp.float32
BF = jnp.bfloat16
LOSS = math.log(0.6)


def mm(a, b):
    return lax.dot_general(a, b, (((1,), (0,)), ((), ())), preferred_element_type=F32)


def mm_nt(a, b):
    return lax.dot_general(a, b, (((1,), (1,)), ((), ())), preferred_element_type=F32)


def mm_tn(a, b):
    return lax.dot_general(a, b, (((0,), (0,)), ((), ())), preferred_element_type=F32)


def iota2(shape, dim):
    return lax.broadcasted_iota(jnp.int32, shape, dim)


def docs_row(docs_ref, block):
    row = docs_ref[pl.ds(block // 2, 1), :].astype(F32)
    odd = jnp.full((1, HALF), block % 2, jnp.int32)
    return jnp.where(odd == 1, row[:, HALF:], row[:, :HALF])


def as_column(row):
    size = row.shape[1]
    eye = iota2((size, size), 0) == iota2((size, size), 1)
    return jnp.sum(jnp.where(eye, jnp.broadcast_to(row, (size, size)), 0.0), axis=1, keepdims=True)


def kda_pairs_kernel(
    place_ref, q_hbm, k_hbm, v_hbm, w_ref, scale_ref, rate_ref, mask_ref, docs_ref,
    lmat, att, rhs, leaving, closing, carried_q,
    q_ref, k_ref, v_ref, sems, qn, kn, vn, acol, wcol, bcol, ccol, tcol, incl, excl,
):
    heads = rate_ref.shape[0]
    place = place_ref[0]
    ranks = docs_ref.shape[0]
    rows = HALF * heads

    copies = [
        pltpu.make_async_copy(source, target, sems.at[n])
        for n, (source, target) in enumerate(((q_hbm, q_ref), (k_hbm, k_ref), (v_hbm, v_ref)))
    ]
    for copy in copies:
        copy.start()

    ti, si = iota2((HALF, HALF), 0), iota2((HALF, HALF), 1)
    scales = scale_ref[...].T
    strengths = w_ref[...].T
    for i in range(2):
        block = place if i == 0 else 2 * ranks - 1 - place
        drow = docs_row(docs_ref, block)
        prior = docs_row(docs_ref, jnp.maximum(block - 1, 0))[:, HALF - 1 :]
        prior = jnp.where(jnp.full((1, 1), block, jnp.int32) > 0, prior, -1.0)
        dcol = as_column(drow)
        same = dcol == drow
        within = jnp.where(same & (ti >= si), 1.0, 0.0)
        incl[i] = within
        excl[i] = jnp.where(same & (ti > si), 1.0, 0.0)
        gates = lax.dot_general(
            within, scales[i * HALF : (i + 1) * HALF, :], (((1,), (0,)), ((), ())),
            precision=lax.Precision.HIGHEST, preferred_element_type=F32,
        )
        lost = mask_ref[:, i * HALF : (i + 1) * HALF].astype(F32)
        bcol[i] = jnp.broadcast_to(jnp.sum(within * lost, axis=1, keepdims=True) * LOSS, (HALF, DN))
        ccol[i] = jnp.broadcast_to(jnp.where(dcol == prior, 1.0, 0.0), (HALF, DN))
        tcol[i] = jnp.broadcast_to(jnp.where(dcol == drow[:, HALF - 1 :], 1.0, 0.0), (HALF, DN))
        writes = strengths[i * HALF : (i + 1) * HALF, :]
        for h in range(heads):
            acol[i * heads + h] = jnp.broadcast_to(gates[:, h : h + 1], (HALF, DN))
            wcol[i * heads + h] = jnp.broadcast_to(writes[:, h : h + 1], (HALF, DN))

    for copy in copies:
        copy.wait()

    def widen(c, _):
        at = pl.ds(pl.multiple_of(c * 256, 256), 256)
        for source, target in ((q_ref, qn), (k_ref, kn)):
            x = source[at, :].astype(F32)
            target[at, :] = x * lax.rsqrt(jnp.sum(x * x, axis=1, keepdims=True) + 1e-06)
        vn[at, :] = v_ref[at, :].astype(F32)
        return 0

    lax.fori_loop(0, 2 * rows // 256, widen, 0)

    def pairs(g, _):
        for u in range(4):
            p = g * 4 + u
            i = p // heads
            h = p % heads
            at = pl.ds(i * rows + h, HALF, stride=heads)
            q, k, v = qn[at, :], kn[at, :], vn[at, :]
            w = wcol[p]
            carried = ccol[i]
            cumlog = bcol[i] - acol[p] * rate_ref[pl.ds(h, 1), :]
            grow = jnp.exp(cumlog)
            kd, qd = k * grow, q * grow
            kg = k * jnp.exp(-cumlog)
            both = jnp.concatenate([kd, qd], axis=0)
            both_hi, kg_hi = both.astype(BF), kg.astype(BF)
            both_lo = (both - both_hi.astype(F32)).astype(BF)
            kg_lo = (kg - kg_hi.astype(F32)).astype(BF)
            inner = mm_nt(both_hi, kg_hi) + mm_nt(both_hi, kg_lo) + mm_nt(both_lo, kg_hi)
            lmat[p] = inner[:HALF] * w[:, :HALF] * excl[i]
            att[p] = (inner[HALF:] * incl[i]).astype(BF)
            rhs[p, :, :DN] = (w * v).astype(BF)
            rhs[p, :, DN:] = (w * carried * kd).astype(BF)
            carried_q[p] = (carried * qd).astype(BF)
            last = grow[HALF - 1 :, :]
            leaving[p] = (kg * last * tcol[i]).astype(BF)
            closing[p] = jnp.broadcast_to(carried[HALF - 1 :, :] * last, (8, DN))
        return 0

    lax.fori_loop(0, 2 * heads // 4, pairs, 0)


def kda_pairs(place, q, k, v, w, scale, rate, mask, docs):
    heads = rate.shape[0]
    n = 2 * heads
    rows = q.shape[0]
    vm = lambda *s: pltpu.VMEM(s, F32)
    spec = pl.BlockSpec(memory_space=pltpu.VMEM)
    shapes = (
        jax.ShapeDtypeStruct((n, HALF, HALF), F32),
        jax.ShapeDtypeStruct((n, HALF, HALF), BF),
        jax.ShapeDtypeStruct((n, HALF, 2 * DN), BF),
        jax.ShapeDtypeStruct((n, HALF, DN), BF),
        jax.ShapeDtypeStruct((n, 8, DN), F32),
        jax.ShapeDtypeStruct((n, HALF, DN), BF),
    )
    return pl.pallas_call(
        kda_pairs_kernel,
        name="kda_pairs",
        out_shape=shapes,
        in_specs=[pl.BlockSpec(memory_space=pltpu.SMEM)]
        + [pl.BlockSpec(memory_space=pltpu.HBM)] * 3
        + [spec] * 5,
        out_specs=(spec,) * 6,
        scratch_shapes=[
            pltpu.VMEM((rows, DN), BF), pltpu.VMEM((rows, DN), BF), pltpu.VMEM((rows, DN), BF),
            pltpu.SemaphoreType.DMA((3,)),
            vm(rows, DN), vm(rows, DN), vm(rows, DN),
            vm(n, HALF, DN), vm(n, HALF, DN),
            vm(2, HALF, DN), vm(2, HALF, DN), vm(2, HALF, DN),
            vm(2, HALF, HALF), vm(2, HALF, HALF),
        ],
        compiler_params=pltpu.CompilerParams(vmem_limit_bytes=32 << 20),
        cost_estimate=pl.CostEstimate(flops=300_000_000, bytes_accessed=12_000_000, transcendentals=600_000),
    )(place, q, k, v, w, scale, rate, mask, docs)


def kda_invert_kernel(lmat, xmat, pick, coef):
    heads = lmat.shape[0] // 2
    ti, si = iota2((HALF, HALF), 0), iota2((HALF, HALF), 1)

    kk, lane = iota2((4 * HALF, DN), 0), iota2((4 * HALF, DN), 1)
    side = (kk // DN) == (lane // HALF)
    for j in range(15):
        pick[:, j * DN : (j + 1) * DN] = jnp.where(side & (kk % 16 == j), 1.0, 0.0).astype(BF)
    near = (ti // 16) == (si // 16)
    rowi, coli = iota2((8, DN), 0), iota2((8, DN), 1) % HALF

    def base(g, _):
        wide = []
        for u in range(4):
            parts = []
            for v in range(2):
                lower = jnp.where(near, lmat[g * 8 + 2 * u + v], 0.0)
                high = lower.astype(BF).astype(F32)
                parts += [high, lower - high]
            wide.append(jnp.concatenate(parts, axis=1).astype(BF))
        coef[...] = mm(jnp.concatenate(wide, axis=0), pick[...])
        for u in range(4):
            made = []
            for b in range(HALF // 16):
                top = jnp.where(coli == rowi + 16 * b, 1.0, 0.0)
                low = jnp.where(coli == rowi + 16 * b + 8, 1.0, 0.0)
                at = u * HALF + 16 * b
                for j in range(15):
                    lanes = slice(j * DN, (j + 1) * DN)
                    row = top[j : j + 1, :] if j < 8 else low[j - 8 : j - 7, :]
                    if j < 7:
                        top = top - coef[at : at + 8, lanes] * row
                    low = low - coef[at + 8 : at + 16, lanes] * row
                made += [top, low]
            x = jnp.concatenate(made, axis=0)
            xmat[g * 8 + 2 * u] = x[:, :HALF]
            xmat[g * 8 + 2 * u + 1] = x[:, HALF:]
        return 0

    lax.fori_loop(0, heads // 4, base, 0)

    def merge(width, g, _):
        tb, sb = ti // width, si // width
        cross = ((tb % 2) == 1) & (sb == tb - 1)
        for u in range(8):
            p = g * 8 + u
            x = xmat[p]
            xb = x.astype(BF)
            y = mm(jnp.where(cross, lmat[p], 0.0).astype(BF), xb)
            xmat[p] = x - mm(xb, y.astype(BF))
        return 0

    lax.fori_loop(0, heads // 4, functools.partial(merge, 16), 0)
    lax.fori_loop(0, heads // 4, functools.partial(merge, 32), 0)


def kda_invert(lmat):
    spec = pl.BlockSpec(memory_space=pltpu.VMEM)
    return pl.pallas_call(
        kda_invert_kernel,
        name="kda_invert",
        out_shape=jax.ShapeDtypeStruct(lmat.shape, F32),
        in_specs=[spec],
        out_specs=spec,
        scratch_shapes=[pltpu.VMEM((4 * HALF, 15 * DN), BF), pltpu.VMEM((4 * HALF, 15 * DN), F32)],
        compiler_params=pltpu.CompilerParams(vmem_limit_bytes=16 << 20),
        cost_estimate=pl.CostEstimate(flops=300_000_000, bytes_accessed=12_000_000, transcendentals=0),
    )(lmat)


def kda_leave_kernel(xmat, rhs, leaving, closing, lat_ref, offs_first, offs_second, tmap, upd):
    heads = xmat.shape[0] // 2
    base_row = heads * DN
    for lb in range(4):
        part = lat_ref[:, lb * DN : (lb + 1) * DN]
        low = base_row + lb * HALF
        offs_first[low : low + HALF, :] = part[:HALF]
        offs_second[low : low + HALF, :] = part[:HALF]
        offs_second[low + 4 * HALF : low + 5 * HALF, :] = part[HALF:]

    def solve(g, _):
        for u in range(8):
            p = g * 8 + u
            upd[p] = mm(xmat[p].astype(BF), rhs[p]).astype(BF)
        return 0

    lax.fori_loop(0, heads // 4, solve, 0)

    eye = iota2((DN, DN), 0) == iota2((DN, DN), 1)
    for i, target in ((0, offs_first), (1, offs_second)):

        def leave(g, _, i=i, target=target):
            for u in range(4):
                h = g * 4 + u
                p = i * heads + h
                made = mm_tn(leaving[p], upd[p])
                target[pl.ds(pl.multiple_of(h * DN, DN), DN), :] = made[:, :DN].astype(BF)
                keep = jnp.where(eye, jnp.broadcast_to(closing[p][:1, :], (DN, DN)), 0.0)
                tmap[p] = (keep - made[:, DN:]).astype(BF)
            return 0

        lax.fori_loop(0, heads // 4, leave, 0)


def kda_leave(xmat, rhs, leaving, closing, latents):
    n = xmat.shape[0]
    spec = pl.BlockSpec(memory_space=pltpu.VMEM)
    shapes = (
        jax.ShapeDtypeStruct((n // 2 * DN + 4 * HALF, DN), BF),
        jax.ShapeDtypeStruct((n // 2 * DN + 8 * HALF, DN), BF),
        jax.ShapeDtypeStruct((n, DN, DN), BF),
        jax.ShapeDtypeStruct((n, HALF, 2 * DN), BF),
    )
    return pl.pallas_call(
        kda_leave_kernel,
        name="kda_leave",
        out_shape=shapes,
        in_specs=[spec] * 5,
        out_specs=(spec,) * 4,
        compiler_params=pltpu.CompilerParams(vmem_limit_bytes=24 << 20),
        cost_estimate=pl.CostEstimate(flops=300_000_000, bytes_accessed=8_000_000, transcendentals=0),
    )(xmat, rhs, leaving, closing, latents)


def kda_local_kernel(att, upd, carried_q, local, squery):
    n = att.shape[0]

    def body(g, _):
        for u in range(8):
            p = g * 8 + u
            made = mm(att[p], upd[p])
            local[p] = made[:, :DN]
            squery[p] = (carried_q[p].astype(F32) - made[:, DN:]).astype(BF)
        return 0

    lax.fori_loop(0, n // 8, body, 0)


def kda_local(att, upd, carried_q):
    n = att.shape[0]
    spec = pl.BlockSpec(memory_space=pltpu.VMEM)
    return pl.pallas_call(
        kda_local_kernel,
        name="kda_local",
        out_shape=(jax.ShapeDtypeStruct((n, HALF, DN), F32), jax.ShapeDtypeStruct((n, HALF, DN), BF)),
        in_specs=[spec] * 3,
        out_specs=(spec,) * 2,
        cost_estimate=pl.CostEstimate(flops=70_000_000, bytes_accessed=4_000_000, transcendentals=0),
    )(att, upd, carried_q)


def kda_carry_kernel(place_ref, tmap, offs_first, offs_second, in_first, in_second, out_first, out_second, *, ranks):
    heads = tmap.shape[0] // 2
    end = jnp.full((DN, DN), place_ref[0], jnp.int32) == ranks - 1
    low = heads * DN
    out_first[low:, :] = in_first[low:, :]
    out_second[low:, :] = in_second[low + 4 * HALF :, :]

    def body(g, _):
        for u in range(4):
            h = g * 4 + u
            at = pl.ds(pl.multiple_of(h * DN, DN), DN)
            own = offs_first[at, :].astype(F32)
            out_first[at, :] = (own + mm(tmap[h], in_first[at, :])).astype(BF)
            upper = jnp.where(end, own, in_second[at, :].astype(F32)).astype(BF)
            out_second[at, :] = (
                offs_second[at, :].astype(F32) + mm(tmap[heads + h], upper)
            ).astype(BF)
        return 0

    lax.fori_loop(0, heads // 4, body, 0)


def kda_carry(place, tmap, offs_first, offs_second, in_first, in_second, ranks):
    spec = pl.BlockSpec(memory_space=pltpu.VMEM)
    shape = jax.ShapeDtypeStruct(offs_first.shape, BF)
    return pl.pallas_call(
        functools.partial(kda_carry_kernel, ranks=ranks),
        name="kda_carry",
        out_shape=(shape, shape),
        in_specs=[pl.BlockSpec(memory_space=pltpu.SMEM)] + [spec] * 5,
        out_specs=(spec, spec),
        cost_estimate=pl.CostEstimate(flops=130_000_000, bytes_accessed=5_000_000, transcendentals=0),
    )(place, tmap, offs_first, offs_second, in_first, in_second)


def kda_close_kernel(place_ref, local, squery, own_first, in_first, in_second, gain, cot_hbm, out_ref, grad_ref, cot_ref, sem, cot, outs, *, ranks):
    heads = local.shape[0] // 2
    rows = HALF * heads
    end = jnp.full((DN, DN), place_ref[0], jnp.int32) == ranks - 1
    copy = pltpu.make_async_copy(cot_hbm, cot_ref, sem)
    copy.start()
    copy.wait()

    def widen(c, _):
        at = pl.ds(pl.multiple_of(c * 256, 256), 256)
        cot[at, :] = cot_ref[at, :].astype(F32)
        return 0

    lax.fori_loop(0, 2 * rows // 256, widen, 0)

    def body(g, grad):
        for u in range(4):
            h = g * 4 + u
            state_at = pl.ds(pl.multiple_of(h * DN, DN), DN)
            upper = jnp.where(
                end, own_first[state_at, :].astype(F32), in_second[state_at, :].astype(F32)
            ).astype(BF)
            for i, state in ((0, in_first[state_at, :]), (1, upper)):
                p = i * heads + h
                raw = local[p] + mm(squery[p], state)
                normed = raw * lax.rsqrt(jnp.mean(raw * raw, axis=1, keepdims=True) + 1e-06)
                at = pl.ds(i * rows + h, HALF, stride=heads)
                outs[at, :] = normed * gain[...]
                terms = normed * cot[at, :]
                grad = grad + jnp.sum(terms.reshape(HALF // 8, 8, DN), axis=0)
        return grad

    grad = lax.fori_loop(0, heads // 4, body, jnp.zeros((8, DN), F32))
    grad_ref[...] = jnp.broadcast_to(jnp.sum(grad, axis=0, keepdims=True), grad_ref.shape)

    def narrow(c, _):
        at = pl.ds(pl.multiple_of(c * 256, 256), 256)
        out_ref[at, :] = outs[at, :].astype(BF)
        return 0

    lax.fori_loop(0, 2 * rows // 256, narrow, 0)


def kda_close(place, local, squery, own_first, in_first, in_second, gain, cot, ranks):
    spec = pl.BlockSpec(memory_space=pltpu.VMEM)
    rows = cot.shape[0]
    return pl.pallas_call(
        functools.partial(kda_close_kernel, ranks=ranks),
        name="kda_close",
        out_shape=(jax.ShapeDtypeStruct((rows, DN), BF), jax.ShapeDtypeStruct((ranks, DN), F32)),
        in_specs=[pl.BlockSpec(memory_space=pltpu.SMEM)] + [spec] * 6 + [pl.BlockSpec(memory_space=pltpu.HBM)],
        out_specs=(spec, spec),
        scratch_shapes=[
            pltpu.VMEM((rows, DN), BF), pltpu.SemaphoreType.DMA,
            pltpu.VMEM((rows, DN), F32), pltpu.VMEM((rows, DN), F32)],
        compiler_params=pltpu.CompilerParams(vmem_limit_bytes=32 << 20),
        cost_estimate=pl.CostEstimate(flops=70_000_000, bytes_accessed=5_000_000, transcendentals=4096),
    )(place, local, squery, own_first, in_first, in_second, gain, cot)


def onehot(shape, source):
    return jnp.where(iota2(shape, 0) == source(iota2(shape, 1)), 1.0, 0.0).astype(BF)


def mla_kernel(
    spot_ref, q_hbm, lat_ref, back_one_hbm, ahead_one_hbm, back_two_hbm, ahead_two_hbm, docs_ref, own_hbm, other_hbm, out_ref,
    q_ref, back_one, ahead_one, back_two, ahead_two, own_w, other_w, sems, qp, keys, keysp, mask, lifted, mixed, outs, *, xs,
):
    ranks = docs_ref.shape[0]
    place, core = spot_ref[0], spot_ref[1]
    heads = q_ref.shape[0] // (2 * HALF)
    low = heads * DN
    quarter = pl.ds(low, 4 * HALF)
    moves = (
        (q_hbm, q_ref),
        (back_two_hbm.at[quarter, :], back_two),
        (back_one_hbm.at[quarter, :], back_one),
        (ahead_two_hbm.at[quarter, :], ahead_two),
        (ahead_one_hbm.at[pl.ds(low, 8 * HALF), :], ahead_one),
        (own_hbm, own_w),
        (other_hbm, other_w),
    )
    copies = [pltpu.make_async_copy(a, b, sems.at[n]) for n, (a, b) in enumerate(moves)]
    for copy in copies:
        copy.start()
    here_z, here_x = place // xs, place % xs
    width = keys.shape[1]

    def piece(ref, at, i, slot):
        for lb in range(4):
            keys[i, slot * HALF : (slot + 1) * HALF, lb * DN : (lb + 1) * DN] = ref[
                at + lb * HALF : at + (lb + 1) * HALF, :
            ]

    keys[0, 3 * HALF :, :] = jnp.zeros((width - 3 * HALF, 4 * DN), BF)
    keys[1, 3 * HALF :, :] = jnp.zeros((width - 3 * HALF, 4 * DN), BF)
    for copy in copies[:5]:
        copy.wait()
    piece(back_two, 0, 0, 0)
    piece(back_one, 0, 0, 1)
    keys[0, 2 * HALF : 3 * HALF, :] = lat_ref[:HALF, :]
    keys[1, 2 * HALF : 3 * HALF, :] = lat_ref[HALF:, :]

    @pl.when(place < ranks - 2)
    def _():
        piece(ahead_two, 0, 1, 0)

    @pl.when(place == ranks - 2)
    def _():
        piece(ahead_one, 0, 1, 0)

    @pl.when(place == ranks - 1)
    def _():
        piece(back_one, 0, 1, 0)
        keys[1, HALF : 2 * HALF, :] = lat_ref[:HALF, :]

    @pl.when(place < ranks - 1)
    def _():
        piece(ahead_one, 4 * HALF, 1, 1)

    def source_n(k):
        off = ((k // 4) % 2) * 4 + ((k // 32) % 2) * 2 + k // 64
        z = lax.bitwise_xor(off, jnp.full(k.shape, here_z, jnp.int32))
        return (z * xs + ((k // 8) % xs + here_x) % xs) * 4 + k % 4

    def source_l(k):
        off = ((k // 16) % 2) * 4 + ((k // 128) % 2) * 2 + k // 256
        z = lax.bitwise_xor(off, jnp.full(k.shape, here_z, jnp.int32))
        return (z * xs + ((k // 32) % xs + here_x) % xs) * 16 + k % 16

    pick = onehot((DN, DN), source_n)
    rows = 256

    def place_q(c, _):
        at = pl.ds(pl.multiple_of(c * rows, rows), rows)
        qp[at, :] = mm(q_ref[at, :], pick)
        return 0

    lax.fori_loop(0, q_ref.shape[0] // rows, place_q, 0)
    spread = onehot((4 * DN, 4 * DN), source_l)
    ti, si = iota2((HALF, HALF), 0), iota2((HALF, HALF), 1)
    for i in range(2):
        keysp[i] = mm(keys[i], spread).astype(BF)
        block = place if i == 0 else 2 * ranks - 1 - place
        drow = docs_row(docs_ref, block)
        dcol = as_column(drow)
        for back in range(3):
            source = block - back
            krow = docs_row(docs_ref, jnp.maximum(source, 0))
            krow = jnp.where(jnp.full((1, HALF), source, jnp.int32) >= 0, krow, -1.0)
            allowed = dcol == krow
            if back == 0:
                allowed = allowed & (ti >= si)
            fill = jnp.where(allowed, 0.0, -1e30)
            for r in range(4):
                mask[i, r * HALF : (r + 1) * HALF, (2 - back) * HALF : (3 - back) * HALF] = fill
        mask[i, :, 3 * HALF :] = jnp.full((4 * HALF, width - 3 * HALF), -1e30, F32)

    span = heads // 2
    for side, weights in ((0, own_w), (1, other_w)):
        first = span * core if side == 0 else span * (1 - core)
        copies[5 + side].wait()

        def lift(g, _, weights=weights, first=first):
            for u in range(2):
                hl = g * 2 + u
                h = first + hl
                q = qp[pl.ds(h, 2 * HALF, stride=heads), :].astype(BF)
                for lb in range(4):
                    at = pl.ds(pl.multiple_of((hl * 4 + lb) * 32, 32), 32)
                    w = jnp.concatenate(
                        [weights[e, b, at, :] for e in range(2) for b in range(2)], axis=0
                    )
                    made = mm(q, w).astype(BF)
                    for i in range(2):
                        dst = pl.ds(pl.multiple_of(h * HALF, HALF), HALF)
                        lifted[i, dst, lb * DN : (lb + 1) * DN] = made[i * HALF : (i + 1) * HALF]
            return 0

        lax.fori_loop(0, span // 2, lift, 0)

    scale = 1.0 / math.sqrt(DN)

    def attend(g, _):
        i = g // (heads // 4)
        at = pl.ds(pl.multiple_of((g % (heads // 4)) * rows, rows), rows)
        logits = mm_nt(lifted[i, at, :], keys[i]) * scale + mask[i]
        peak = jnp.max(logits, axis=1, keepdims=True)
        expo = jnp.exp(logits - peak)
        probs = (expo / jnp.sum(expo, axis=1, keepdims=True)).astype(BF)
        mixed[i, at, :] = mm(probs, keysp[i]).astype(BF)
        return 0

    lax.fori_loop(0, heads // 2, attend, 0)

    for side, weights in ((0, own_w), (1, other_w)):
        first = span * core if side == 0 else span * (1 - core)

        def lower(g, _, weights=weights, first=first):
            for u in range(2):
                hl = g * 2 + u
                h = first + hl
                w = jnp.concatenate(
                    [
                        weights[e, b, pl.ds(pl.multiple_of(1024 + (c * span + hl) * 16, 16), 16), :]
                        for e in range(2) for b in range(2) for c in range(8)
                    ],
                    axis=0,
                )
                src = pl.ds(pl.multiple_of(h * HALF, HALF), HALF)
                both = jnp.concatenate([mixed[0, src, :], mixed[1, src, :]], axis=0)
                outs[pl.ds(h, 2 * HALF, stride=heads), :] = mm(both, w)
            return 0

        lax.fori_loop(0, span // 2, lower, 0)

    def narrow(c, _):
        at = pl.ds(pl.multiple_of(c * rows, rows), rows)
        out_ref[at, :] = outs[at, :].astype(BF)
        return 0

    lax.fori_loop(0, q_ref.shape[0] // rows, narrow, 0)


def mla(spot, q, latents, back_one, ahead_one, back_two, ahead_two, docs, own_w, other_w, xs):
    spec = pl.BlockSpec(memory_space=pltpu.VMEM)
    hbm = pl.BlockSpec(memory_space=pltpu.HBM)
    rows = q.shape[0]
    return pl.pallas_call(
        functools.partial(mla_kernel, xs=xs),
        name="mla",
        out_shape=jax.ShapeDtypeStruct((rows, DN), BF),
        in_specs=[pl.BlockSpec(memory_space=pltpu.SMEM), hbm, spec, hbm, hbm, hbm, hbm, spec, hbm, hbm],
        out_specs=spec,
        scratch_shapes=[
            pltpu.VMEM((rows, DN), BF),
            pltpu.VMEM((4 * HALF, DN), BF),
            pltpu.VMEM((8 * HALF, DN), BF),
            pltpu.VMEM((4 * HALF, DN), BF),
            pltpu.VMEM((4 * HALF, DN), BF),
            pltpu.VMEM(own_w.shape, BF),
            pltpu.VMEM(own_w.shape, BF),
            pltpu.SemaphoreType.DMA((7,)),
            pltpu.VMEM((rows, DN), F32),
            pltpu.VMEM((2, 256, 4 * DN), BF),
            pltpu.VMEM((2, 256, 4 * DN), BF),
            pltpu.VMEM((2, 256, 256), F32),
            pltpu.VMEM((2, rows // 2, 4 * DN), BF),
            pltpu.VMEM((2, rows // 2, 4 * DN), BF),
            pltpu.VMEM((rows, DN), F32),
        ],
        compiler_params=pltpu.CompilerParams(vmem_limit_bytes=60 << 20),
        cost_estimate=pl.CostEstimate(flops=1_500_000_000, bytes_accessed=7_000_000, transcendentals=600_000),
    )(spot, q, latents, back_one, ahead_one, back_two, ahead_two, docs, own_w, other_w)


def from_behind(value, axis, steps):
    count = lax.axis_size(axis)
    leading, last = (max(0, -steps), min(count, count - steps))
    return lax.ppermute(value, axis, [(source, source + steps) for source in range(leading, last)])


def shards(
    delta_query_rows,
    delta_key_rows,
    delta_value_rows,
    delta_write_strength,
    token_gate_scale,
    channel_decay_rate,
    sudden_loss_mask,
    document_numbers,
    delta_norm_gain,
    delta_output_cotangent,
    latent_query_rows,
    compressed_latents,
    query_to_latent_map,
    latent_to_value_map,
):
    ranks = lax.axis_size("ctx")
    place = lax.axis_index("ctx")
    seqs = delta_query_rows.shape[0]
    rows = delta_query_rows.shape[1]
    heads = delta_query_rows.shape[2]
    value_width = delta_value_rows.shape[3]
    here = place.astype(jnp.int32).reshape(1)
    docs = document_numbers.reshape(ranks, rows)
    latents = compressed_latents[0]
    flat = lambda tensor: tensor.reshape(rows * heads, tensor.shape[3])

    groups = lax.axis_size("dp")
    member = lax.axis_index("dp")
    core = member % 2
    span = heads // 2
    keep_lift = lax.dynamic_slice_in_dim(query_to_latent_map, core * span, span, 0)
    keep_lower = lax.dynamic_slice_in_dim(latent_to_value_map, core * span, span, 0)
    lift_rows = keep_lift.reshape(span, 4, 4, DN).transpose(0, 2, 1, 3).reshape(span * 16, DN)
    held = jnp.concatenate([lift_rows, keep_lower.reshape(span * 16, DN)], axis=0)

    def across(value, step):
        return lax.ppermute(value, "ctx", [(i, i ^ step) for i in range(ranks)])

    held = jnp.stack([held, across(held, 4 * XS)])
    columns = [held]
    for step in range(1, XS):
        pairs = [(i - i % XS + (i + step) % XS, i) for i in range(ranks)]
        columns.append(lax.ppermute(held, "ctx", pairs))
    held = jnp.stack(columns)
    lift_tiles = held[:, :, : span * 16].reshape(XS, 2, span, 4, 4, DN)
    lift_tiles = lift_tiles.transpose(2, 3, 0, 1, 4, 5).reshape(span * 128, DN)
    held = jnp.concatenate([lift_tiles, held[:, :, span * 16 :].reshape(span * 128, DN)], axis=0)
    held = jnp.stack([held, across(held, 2 * XS)])
    own_w = jnp.stack([held, across(held, XS)])
    other_w = lax.ppermute(own_w, "dp", [(i, i ^ 1) for i in range(groups)])

    lmat, att, rhs, leaving, closing, carried_q = kda_pairs(
        here,
        flat(delta_query_rows),
        flat(delta_key_rows),
        flat(delta_value_rows),
        delta_write_strength[0].T,
        token_gate_scale[0].T,
        channel_decay_rate,
        sudden_loss_mask,
        docs,
    )
    xmat = kda_invert(lmat)
    offs_first, offs_second, tmap, upd = kda_leave(xmat, rhs, leaving, closing, latents)
    near_first = from_behind(offs_first, "ctx", 1)
    near_second = from_behind(offs_second, "ctx", -1)
    local, squery = kda_local(att, upd, carried_q)
    out_first, out_second = kda_carry(
        here, tmap, offs_first, offs_second, near_first, near_second, ranks
    )
    far_first = from_behind(out_first, "ctx", 1)
    far_second = from_behind(out_second, "ctx", -1)
    normed_rows, partial_grad = kda_close(
        here,
        local,
        squery,
        out_first,
        far_first,
        far_second,
        delta_norm_gain.reshape(1, value_width),
        flat(delta_output_cotangent),
        ranks,
    )
    kda_output = normed_rows.reshape(seqs, rows, heads, value_width)
    terms = lax.all_to_all(partial_grad, "ctx", 0, 0, tiled=True)
    spread = jnp.broadcast_to(jnp.sum(terms, axis=0), (groups, value_width))
    terms = lax.all_to_all(spread, "dp", 0, 0, tiled=True)
    total_grad = jnp.sum(terms, axis=0)
    gain_grad = total_grad / math.sqrt(seqs * groups * rows * ranks * heads)

    spot = jnp.stack([place, core]).astype(jnp.int32)
    mla_rows = mla(
        spot,
        flat(latent_query_rows),
        latents,
        near_first,
        near_second,
        far_first,
        far_second,
        docs,
        own_w,
        other_w,
        XS,
    )
    mla_output = mla_rows.reshape(seqs, rows, heads, DN)
    return (kda_output, mla_output, gain_grad)


def solution(mesh):
    placed = (
        P("dp", "ctx", None, None),
        P("dp", "ctx", None, None),
        P("dp", "ctx", None, None),
        P("dp", "ctx", None),
        P("dp", "ctx", None),
        P(),
        P("dp", "ctx"),
        P("dp", None),
        P(),
        P("dp", "ctx", None, None),
        P("dp", "ctx", None, None),
        P("dp", "ctx", None),
        P(None, "ctx", None),
        P(None, "ctx", None),
    )
    return jax.shard_map(
        shards,
        mesh=mesh,
        in_specs=placed,
        out_specs=(P("dp", "ctx", None, None), P("dp", "ctx", None, None), P()),
        check_vma=False,
    )
```

```python
import functools
import math

import jax
import jax.numpy as jnp
from jax import lax
from jax.experimental import pallas as pl
from jax.experimental.pallas import tpu as pltpu
from jax.sharding import PartitionSpec as P

DN = 128
XS = 4
HALF = 64
F32 = jnp.float32
BF = jnp.bfloat16
LOSS = math.log(0.6)


def mm(a, b):
    return lax.dot_general(a, b, (((1,), (0,)), ((), ())), preferred_element_type=F32)


def mm_nt(a, b):
    return lax.dot_general(a, b, (((1,), (1,)), ((), ())), preferred_element_type=F32)


def mm_tn(a, b):
    return lax.dot_general(a, b, (((0,), (0,)), ((), ())), preferred_element_type=F32)


def iota2(shape, dim):
    return lax.broadcasted_iota(jnp.int32, shape, dim)


def docs_row(docs_ref, block):
    row = docs_ref[pl.ds(block // 2, 1), :].astype(F32)
    odd = jnp.full((1, HALF), block % 2, jnp.int32)
    return jnp.where(odd == 1, row[:, HALF:], row[:, :HALF])


def as_column(row):
    size = row.shape[1]
    eye = iota2((size, size), 0) == iota2((size, size), 1)
    return jnp.sum(jnp.where(eye, jnp.broadcast_to(row, (size, size)), 0.0), axis=1, keepdims=True)


def kda_pairs_kernel(
    place_ref, q_hbm, k_hbm, v_hbm, w_ref, scale_ref, rate_ref, mask_ref, docs_ref,
    lmat, att, rhs, leaving, closing, carried_q,
    q_ref, k_ref, v_ref, sems, qn, kn, vn, acol, wcol, bcol, ccol, tcol, incl, excl,
):
    heads = rate_ref.shape[0]
    place = place_ref[0]
    ranks = docs_ref.shape[0]
    rows = HALF * heads

    copies = [
        pltpu.make_async_copy(source, target, sems.at[n])
        for n, (source, target) in enumerate(((q_hbm, q_ref), (k_hbm, k_ref), (v_hbm, v_ref)))
    ]
    for copy in copies:
        copy.start()

    ti, si = iota2((HALF, HALF), 0), iota2((HALF, HALF), 1)
    scales = scale_ref[...].T
    strengths = w_ref[...].T
    for i in range(2):
        block = place if i == 0 else 2 * ranks - 1 - place
        drow = docs_row(docs_ref, block)
        prior = docs_row(docs_ref, jnp.maximum(block - 1, 0))[:, HALF - 1 :]
        prior = jnp.where(jnp.full((1, 1), block, jnp.int32) > 0, prior, -1.0)
        dcol = as_column(drow)
        same = dcol == drow
        within = jnp.where(same & (ti >= si), 1.0, 0.0)
        incl[i] = within
        excl[i] = jnp.where(same & (ti > si), 1.0, 0.0)
        gates = lax.dot_general(
            within, scales[i * HALF : (i + 1) * HALF, :], (((1,), (0,)), ((), ())),
            precision=lax.Precision.HIGHEST, preferred_element_type=F32,
        )
        lost = mask_ref[:, i * HALF : (i + 1) * HALF].astype(F32)
        bcol[i] = jnp.broadcast_to(jnp.sum(within * lost, axis=1, keepdims=True) * LOSS, (HALF, DN))
        ccol[i] = jnp.broadcast_to(jnp.where(dcol == prior, 1.0, 0.0), (HALF, DN))
        tcol[i] = jnp.broadcast_to(jnp.where(dcol == drow[:, HALF - 1 :], 1.0, 0.0), (HALF, DN))
        writes = strengths[i * HALF : (i + 1) * HALF, :]
        for h in range(heads):
            acol[i * heads + h] = jnp.broadcast_to(gates[:, h : h + 1], (HALF, DN))
            wcol[i * heads + h] = jnp.broadcast_to(writes[:, h : h + 1], (HALF, DN))

    for copy in copies:
        copy.wait()

    def widen(c, _):
        at = pl.ds(pl.multiple_of(c * 256, 256), 256)
        for source, target in ((q_ref, qn), (k_ref, kn)):
            x = source[at, :].astype(F32)
            target[at, :] = x * lax.rsqrt(jnp.sum(x * x, axis=1, keepdims=True) + 1e-06)
        vn[at, :] = v_ref[at, :].astype(F32)
        return 0

    lax.fori_loop(0, 2 * rows // 256, widen, 0)

    def pairs(g, _):
        for u in range(4):
            p = g * 4 + u
            i = p // heads
            h = p % heads
            at = pl.ds(i * rows + h, HALF, stride=heads)
            q, k, v = qn[at, :], kn[at, :], vn[at, :]
            w = wcol[p]
            carried = ccol[i]
            cumlog = bcol[i] - acol[p] * rate_ref[pl.ds(h, 1), :]
            grow = jnp.exp(cumlog)
            kd, qd = k * grow, q * grow
            kg = k * jnp.exp(-cumlog)
            both = jnp.concatenate([kd, qd], axis=0)
            both_hi, kg_hi = both.astype(BF), kg.astype(BF)
            both_lo = (both - both_hi.astype(F32)).astype(BF)
            kg_lo = (kg - kg_hi.astype(F32)).astype(BF)
            inner = mm_nt(both_hi, kg_hi) + mm_nt(both_hi, kg_lo) + mm_nt(both_lo, kg_hi)
            lmat[p] = inner[:HALF] * w[:, :HALF] * excl[i]
            att[p] = (inner[HALF:] * incl[i]).astype(BF)
            rhs[p, :, :DN] = (w * v).astype(BF)
            rhs[p, :, DN:] = (w * carried * kd).astype(BF)
            carried_q[p] = (carried * qd).astype(BF)
            last = grow[HALF - 1 :, :]
            leaving[p] = (kg * last * tcol[i]).astype(BF)
            closing[p] = jnp.broadcast_to(carried[HALF - 1 :, :] * last, (8, DN))
        return 0

    lax.fori_loop(0, 2 * heads // 4, pairs, 0)


def kda_pairs(place, q, k, v, w, scale, rate, mask, docs):
    heads = rate.shape[0]
    n = 2 * heads
    rows = q.shape[0]
    vm = lambda *s: pltpu.VMEM(s, F32)
    spec = pl.BlockSpec(memory_space=pltpu.VMEM)
    shapes = (
        jax.ShapeDtypeStruct((n, HALF, HALF), F32),
        jax.ShapeDtypeStruct((n, HALF, HALF), BF),
        jax.ShapeDtypeStruct((n, HALF, 2 * DN), BF),
        jax.ShapeDtypeStruct((n, HALF, DN), BF),
        jax.ShapeDtypeStruct((n, 8, DN), F32),
        jax.ShapeDtypeStruct((n, HALF, DN), BF),
    )
    return pl.pallas_call(
        kda_pairs_kernel,
        name="kda_pairs",
        out_shape=shapes,
        in_specs=[pl.BlockSpec(memory_space=pltpu.SMEM)]
        + [pl.BlockSpec(memory_space=pltpu.HBM)] * 3
        + [spec] * 5,
        out_specs=(spec,) * 6,
        scratch_shapes=[
            pltpu.VMEM((rows, DN), BF), pltpu.VMEM((rows, DN), BF), pltpu.VMEM((rows, DN), BF),
            pltpu.SemaphoreType.DMA((3,)),
            vm(rows, DN), vm(rows, DN), vm(rows, DN),
            vm(n, HALF, DN), vm(n, HALF, DN),
            vm(2, HALF, DN), vm(2, HALF, DN), vm(2, HALF, DN),
            vm(2, HALF, HALF), vm(2, HALF, HALF),
        ],
        compiler_params=pltpu.CompilerParams(vmem_limit_bytes=60 << 20),
        cost_estimate=pl.CostEstimate(flops=300_000_000, bytes_accessed=12_000_000, transcendentals=600_000),
    )(place, q, k, v, w, scale, rate, mask, docs)


def kda_invert_kernel(lmat, xmat, pick, coef):
    heads = lmat.shape[0] // 2
    ti, si = iota2((HALF, HALF), 0), iota2((HALF, HALF), 1)

    kk, lane = iota2((4 * HALF, DN), 0), iota2((4 * HALF, DN), 1)
    side = (kk // DN) == (lane // HALF)
    for j in range(15):
        pick[:, j * DN : (j + 1) * DN] = jnp.where(side & (kk % 16 == j), 1.0, 0.0).astype(BF)
    near = (ti // 16) == (si // 16)
    rowi, coli = iota2((8, DN), 0), iota2((8, DN), 1) % HALF

    def base(g, _):
        wide = []
        for u in range(4):
            parts = []
            for v in range(2):
                lower = jnp.where(near, lmat[g * 8 + 2 * u + v], 0.0)
                high = lower.astype(BF).astype(F32)
                parts += [high, lower - high]
            wide.append(jnp.concatenate(parts, axis=1).astype(BF))
        coef[...] = mm(jnp.concatenate(wide, axis=0), pick[...])
        for u in range(4):
            made = []
            for b in range(HALF // 16):
                top = jnp.where(coli == rowi + 16 * b, 1.0, 0.0)
                low = jnp.where(coli == rowi + 16 * b + 8, 1.0, 0.0)
                at = u * HALF + 16 * b
                for j in range(15):
                    lanes = slice(j * DN, (j + 1) * DN)
                    row = top[j : j + 1, :] if j < 8 else low[j - 8 : j - 7, :]
                    if j < 7:
                        top = top - coef[at : at + 8, lanes] * row
                    low = low - coef[at + 8 : at + 16, lanes] * row
                made += [top, low]
            x = jnp.concatenate(made, axis=0)
            xmat[g * 8 + 2 * u] = x[:, :HALF]
            xmat[g * 8 + 2 * u + 1] = x[:, HALF:]
        return 0

    lax.fori_loop(0, heads // 4, base, 0)

    def merge(width, g, _):
        tb, sb = ti // width, si // width
        cross = ((tb % 2) == 1) & (sb == tb - 1)
        for u in range(8):
            p = g * 8 + u
            x = xmat[p]
            xb = x.astype(BF)
            y = mm(jnp.where(cross, lmat[p], 0.0).astype(BF), xb)
            xmat[p] = x - mm(xb, y.astype(BF))
        return 0

    lax.fori_loop(0, heads // 4, functools.partial(merge, 16), 0)
    lax.fori_loop(0, heads // 4, functools.partial(merge, 32), 0)


def kda_invert(lmat):
    spec = pl.BlockSpec(memory_space=pltpu.VMEM)
    return pl.pallas_call(
        kda_invert_kernel,
        name="kda_invert",
        out_shape=jax.ShapeDtypeStruct(lmat.shape, F32),
        in_specs=[spec],
        out_specs=spec,
        scratch_shapes=[pltpu.VMEM((4 * HALF, 15 * DN), BF), pltpu.VMEM((4 * HALF, 15 * DN), F32)],
        compiler_params=pltpu.CompilerParams(vmem_limit_bytes=16 << 20),
        cost_estimate=pl.CostEstimate(flops=300_000_000, bytes_accessed=12_000_000, transcendentals=0),
    )(lmat)


def kda_leave_kernel(xmat, rhs, leaving, closing, offs_first, offs_second, tmap, upd):
    heads = xmat.shape[0] // 2

    def solve(g, _):
        for u in range(8):
            p = g * 8 + u
            upd[p] = mm(xmat[p].astype(BF), rhs[p]).astype(BF)
        return 0

    lax.fori_loop(0, heads // 4, solve, 0)

    eye = iota2((DN, DN), 0) == iota2((DN, DN), 1)
    for i, target in ((0, offs_first), (1, offs_second)):

        def leave(g, _, i=i, target=target):
            for u in range(4):
                h = g * 4 + u
                p = i * heads + h
                made = mm_tn(leaving[p], upd[p])
                target[pl.ds(pl.multiple_of(h * DN, DN), DN), :] = made[:, :DN].astype(BF)
                keep = jnp.where(eye, jnp.broadcast_to(closing[p][:1, :], (DN, DN)), 0.0)
                tmap[p] = (keep - made[:, DN:]).astype(BF)
            return 0

        lax.fori_loop(0, heads // 4, leave, 0)


def kda_leave(xmat, rhs, leaving, closing):
    n = xmat.shape[0]
    spec = pl.BlockSpec(memory_space=pltpu.VMEM)
    shapes = (
        jax.ShapeDtypeStruct((n // 2 * DN, DN), BF),
        jax.ShapeDtypeStruct((n // 2 * DN, DN), BF),
        jax.ShapeDtypeStruct((n, DN, DN), BF),
        jax.ShapeDtypeStruct((n, HALF, 2 * DN), BF),
    )
    return pl.pallas_call(
        kda_leave_kernel,
        name="kda_leave",
        out_shape=shapes,
        in_specs=[spec] * 4,
        out_specs=(spec,) * 4,
        compiler_params=pltpu.CompilerParams(vmem_limit_bytes=24 << 20),
        cost_estimate=pl.CostEstimate(flops=300_000_000, bytes_accessed=8_000_000, transcendentals=0),
    )(xmat, rhs, leaving, closing)


def kda_local_kernel(att, upd, carried_q, local, squery):
    n = att.shape[0]

    def body(g, _):
        for u in range(8):
            p = g * 8 + u
            made = mm(att[p], upd[p])
            local[p] = made[:, :DN]
            squery[p] = (carried_q[p].astype(F32) - made[:, DN:]).astype(BF)
        return 0

    lax.fori_loop(0, n // 8, body, 0)


def kda_local(att, upd, carried_q):
    n = att.shape[0]
    spec = pl.BlockSpec(memory_space=pltpu.VMEM)
    return pl.pallas_call(
        kda_local_kernel,
        name="kda_local",
        out_shape=(jax.ShapeDtypeStruct((n, HALF, DN), F32), jax.ShapeDtypeStruct((n, HALF, DN), BF)),
        in_specs=[spec] * 3,
        out_specs=(spec,) * 2,
        cost_estimate=pl.CostEstimate(flops=70_000_000, bytes_accessed=4_000_000, transcendentals=0),
    )(att, upd, carried_q)


def kda_carry_kernel(place_ref, tmap, offs_first, offs_second, in_first, in_second, out_first, out_second, *, ranks):
    heads = tmap.shape[0] // 2
    end = jnp.full((DN, DN), place_ref[0], jnp.int32) == ranks - 1

    def body(g, _):
        for u in range(4):
            h = g * 4 + u
            at = pl.ds(pl.multiple_of(h * DN, DN), DN)
            own = offs_first[at, :].astype(F32)
            out_first[at, :] = (own + mm(tmap[h], in_first[at, :])).astype(BF)
            upper = jnp.where(end, own, in_second[at, :].astype(F32)).astype(BF)
            out_second[at, :] = (
                offs_second[at, :].astype(F32) + mm(tmap[heads + h], upper)
            ).astype(BF)
        return 0

    lax.fori_loop(0, heads // 4, body, 0)


def kda_carry(place, tmap, offs_first, offs_second, in_first, in_second, ranks):
    spec = pl.BlockSpec(memory_space=pltpu.VMEM)
    shape = jax.ShapeDtypeStruct(offs_first.shape, BF)
    return pl.pallas_call(
        functools.partial(kda_carry_kernel, ranks=ranks),
        name="kda_carry",
        out_shape=(shape, shape),
        in_specs=[pl.BlockSpec(memory_space=pltpu.SMEM)] + [spec] * 5,
        out_specs=(spec, spec),
        cost_estimate=pl.CostEstimate(flops=130_000_000, bytes_accessed=5_000_000, transcendentals=0),
    )(place, tmap, offs_first, offs_second, in_first, in_second)


def kda_close_kernel(place_ref, local, squery, own_first, in_first, in_second, gain, cot_hbm, out_ref, grad_ref, cot_ref, sem, cot, outs, *, ranks):
    heads = local.shape[0] // 2
    rows = HALF * heads
    end = jnp.full((DN, DN), place_ref[0], jnp.int32) == ranks - 1
    copy = pltpu.make_async_copy(cot_hbm, cot_ref, sem)
    copy.start()
    copy.wait()

    def widen(c, _):
        at = pl.ds(pl.multiple_of(c * 256, 256), 256)
        cot[at, :] = cot_ref[at, :].astype(F32)
        return 0

    lax.fori_loop(0, 2 * rows // 256, widen, 0)

    def body(g, grad):
        for u in range(4):
            h = g * 4 + u
            state_at = pl.ds(pl.multiple_of(h * DN, DN), DN)
            upper = jnp.where(
                end, own_first[state_at, :].astype(F32), in_second[state_at, :].astype(F32)
            ).astype(BF)
            for i, state in ((0, in_first[state_at, :]), (1, upper)):
                p = i * heads + h
                raw = local[p] + mm(squery[p], state)
                normed = raw * lax.rsqrt(jnp.mean(raw * raw, axis=1, keepdims=True) + 1e-06)
                at = pl.ds(i * rows + h, HALF, stride=heads)
                outs[at, :] = normed * gain[...]
                terms = normed * cot[at, :]
                grad = grad + jnp.sum(terms.reshape(HALF // 8, 8, DN), axis=0)
        return grad

    grad = lax.fori_loop(0, heads // 4, body, jnp.zeros((8, DN), F32))
    grad_ref[...] = jnp.broadcast_to(jnp.sum(grad, axis=0, keepdims=True), grad_ref.shape)

    def narrow(c, _):
        at = pl.ds(pl.multiple_of(c * 256, 256), 256)
        out_ref[at, :] = outs[at, :].astype(BF)
        return 0

    lax.fori_loop(0, 2 * rows // 256, narrow, 0)


def kda_close(place, local, squery, own_first, in_first, in_second, gain, cot, ranks):
    spec = pl.BlockSpec(memory_space=pltpu.VMEM)
    rows = cot.shape[0]
    return pl.pallas_call(
        functools.partial(kda_close_kernel, ranks=ranks),
        name="kda_close",
        out_shape=(jax.ShapeDtypeStruct((rows, DN), BF), jax.ShapeDtypeStruct((ranks, DN), F32)),
        in_specs=[pl.BlockSpec(memory_space=pltpu.SMEM)] + [spec] * 6 + [pl.BlockSpec(memory_space=pltpu.HBM)],
        out_specs=(spec, spec),
        scratch_shapes=[
            pltpu.VMEM((rows, DN), BF), pltpu.SemaphoreType.DMA,
            pltpu.VMEM((rows, DN), F32), pltpu.VMEM((rows, DN), F32)],
        compiler_params=pltpu.CompilerParams(vmem_limit_bytes=32 << 20),
        cost_estimate=pl.CostEstimate(flops=70_000_000, bytes_accessed=5_000_000, transcendentals=4096),
    )(place, local, squery, own_first, in_first, in_second, gain, cot)


def onehot(shape, source):
    return jnp.where(iota2(shape, 0) == source(iota2(shape, 1)), 1.0, 0.0).astype(BF)


def mla_kernel(
    spot_ref, q_hbm, lat_ref, back_one_hbm, ahead_one_hbm, back_two_hbm, ahead_two_hbm, docs_ref, own_hbm, other_hbm, out_ref,
    q_ref, back_one, ahead_one, back_two, ahead_two, own_w, other_w, sems, qp, keys, keysp, mask, lifted, mixed, outs, *, xs,
):
    ranks = docs_ref.shape[0]
    place, core = spot_ref[0], spot_ref[1]
    heads = q_ref.shape[0] // (2 * HALF)
    moves = (
        (q_hbm, q_ref),
        (back_two_hbm.at[pl.ds(4 * HALF, 4 * HALF), :], back_two),
        (back_one_hbm.at[pl.ds(8 * HALF, 4 * HALF), :], back_one),
        (ahead_two_hbm.at[pl.ds(4 * HALF, 4 * HALF), :], ahead_two),
        (ahead_one_hbm.at[pl.ds(8 * HALF, 8 * HALF), :], ahead_one),
        (own_hbm, own_w),
        (other_hbm, other_w),
    )
    copies = [pltpu.make_async_copy(a, b, sems.at[n]) for n, (a, b) in enumerate(moves)]
    for copy in copies:
        copy.start()
    width = keys.shape[1]

    def piece(ref, at, i, slot):
        for lb in range(4):
            keys[i, slot * HALF : (slot + 1) * HALF, lb * DN : (lb + 1) * DN] = ref[
                at + lb * HALF : at + (lb + 1) * HALF, :
            ]

    keys[0, 3 * HALF :, :] = jnp.zeros((width - 3 * HALF, 4 * DN), BF)
    keys[1, 3 * HALF :, :] = jnp.zeros((width - 3 * HALF, 4 * DN), BF)
    for copy in copies[:5]:
        copy.wait()
    piece(back_two, 0, 0, 0)
    piece(back_one, 0, 0, 1)
    keys[0, 2 * HALF : 3 * HALF, :] = lat_ref[:HALF, :]
    keys[1, 2 * HALF : 3 * HALF, :] = lat_ref[HALF:, :]

    @pl.when(place < ranks - 2)
    def _():
        piece(ahead_two, 0, 1, 0)

    @pl.when(place == ranks - 2)
    def _():
        piece(ahead_one, 0, 1, 0)

    @pl.when(place == ranks - 1)
    def _():
        piece(back_one, 0, 1, 0)
        keys[1, HALF : 2 * HALF, :] = lat_ref[:HALF, :]

    @pl.when(place < ranks - 1)
    def _():
        piece(ahead_one, 4 * HALF, 1, 1)

    def source_n(k):
        turn, column = k // 64 + 2 * ((k // 32) % 2) + 4 * ((k // 4) % 2), (k // 8) % xs
        shift = jnp.where(column == xs - 1, -1, column) + xs * turn
        return ((shift + place + ranks) % ranks) * 4 + k % 4

    def source_l(k):
        turn, column = 7 * (k // 256) + 6 * ((k // 128) % 2) + 4 * ((k // 16) % 2), (k // 32) % xs
        shift = jnp.where(column >= xs // 2, column - xs, column) + xs * turn
        return ((shift + place + ranks) % ranks) * 16 + k % 16

    pick = onehot((DN, DN), source_n)
    rows = 256

    def place_q(c, _):
        at = pl.ds(pl.multiple_of(c * rows, rows), rows)
        qp[at, :] = mm(q_ref[at, :], pick)
        return 0

    lax.fori_loop(0, q_ref.shape[0] // rows, place_q, 0)
    spread = onehot((4 * DN, 4 * DN), source_l)
    ti, si = iota2((HALF, HALF), 0), iota2((HALF, HALF), 1)
    for i in range(2):
        keysp[i] = mm(keys[i], spread).astype(BF)
        block = place if i == 0 else 2 * ranks - 1 - place
        drow = docs_row(docs_ref, block)
        dcol = as_column(drow)
        for back in range(3):
            source = block - back
            krow = docs_row(docs_ref, jnp.maximum(source, 0))
            krow = jnp.where(jnp.full((1, HALF), source, jnp.int32) >= 0, krow, -1.0)
            allowed = dcol == krow
            if back == 0:
                allowed = allowed & (ti >= si)
            fill = jnp.where(allowed, 0.0, -1e30)
            for r in range(4):
                mask[i, r * HALF : (r + 1) * HALF, (2 - back) * HALF : (3 - back) * HALF] = fill
        mask[i, :, 3 * HALF :] = jnp.full((4 * HALF, width - 3 * HALF), -1e30, F32)

    span = heads // 2
    for side, weights in ((0, own_w), (1, other_w)):
        first = span * core if side == 0 else span * (1 - core)
        copies[5 + side].wait()

        def lift(g, _, weights=weights, first=first):
            for u in range(2):
                hl = g * 2 + u
                h = first + hl
                q = qp[pl.ds(h, 2 * HALF, stride=heads), :].astype(BF)
                for lb in range(4):
                    at = pl.ds(pl.multiple_of((hl * 4 + lb) * 32, 32), 32)
                    w = jnp.concatenate(
                        [weights[0, e, b, at, :] for e in range(2) for b in range(2)], axis=0
                    )
                    made = mm(q, w).astype(BF)
                    for i in range(2):
                        dst = pl.ds(pl.multiple_of(h * HALF, HALF), HALF)
                        lifted[i, dst, lb * DN : (lb + 1) * DN] = made[i * HALF : (i + 1) * HALF]
            return 0

        lax.fori_loop(0, span // 2, lift, 0)

    scale = 1.0 / math.sqrt(DN)

    def attend(g, _):
        i = g // (heads // 4)
        at = pl.ds(pl.multiple_of((g % (heads // 4)) * rows, rows), rows)
        logits = mm_nt(lifted[i, at, :], keys[i]) * scale + mask[i]
        peak = jnp.max(logits, axis=1, keepdims=True)
        expo = jnp.exp(logits - peak)
        probs = (expo / jnp.sum(expo, axis=1, keepdims=True)).astype(BF)
        mixed[i, at, :] = mm(probs, keysp[i]).astype(BF)
        return 0

    lax.fori_loop(0, heads // 2, attend, 0)

    for side, weights in ((0, own_w), (1, other_w)):
        first = span * core if side == 0 else span * (1 - core)

        def lower(g, _, weights=weights, first=first):
            for u in range(2):
                hl = g * 2 + u
                h = first + hl
                w = jnp.concatenate(
                    [
                        weights[1, e, b, pl.ds(pl.multiple_of((c * span + hl) * 16, 16), 16), :]
                        for e in range(2) for b in range(2) for c in range(8)
                    ],
                    axis=0,
                )
                src = pl.ds(pl.multiple_of(h * HALF, HALF), HALF)
                both = jnp.concatenate([mixed[0, src, :], mixed[1, src, :]], axis=0)
                outs[pl.ds(h, 2 * HALF, stride=heads), :] = mm(both, w)
            return 0

        lax.fori_loop(0, span // 2, lower, 0)

    def narrow(c, _):
        at = pl.ds(pl.multiple_of(c * rows, rows), rows)
        out_ref[at, :] = outs[at, :].astype(BF)
        return 0

    lax.fori_loop(0, q_ref.shape[0] // rows, narrow, 0)


def mla(spot, q, latents, back_one, ahead_one, back_two, ahead_two, docs, own_w, other_w, xs):
    spec = pl.BlockSpec(memory_space=pltpu.VMEM)
    hbm = pl.BlockSpec(memory_space=pltpu.HBM)
    rows = q.shape[0]
    return pl.pallas_call(
        functools.partial(mla_kernel, xs=xs),
        name="mla",
        out_shape=jax.ShapeDtypeStruct((rows, DN), BF),
        in_specs=[pl.BlockSpec(memory_space=pltpu.SMEM), hbm, spec, hbm, hbm, hbm, hbm, spec, hbm, hbm],
        out_specs=spec,
        scratch_shapes=[
            pltpu.VMEM((rows, DN), BF),
            pltpu.VMEM((4 * HALF, DN), BF),
            pltpu.VMEM((8 * HALF, DN), BF),
            pltpu.VMEM((4 * HALF, DN), BF),
            pltpu.VMEM((4 * HALF, DN), BF),
            pltpu.VMEM(own_w.shape, BF),
            pltpu.VMEM(own_w.shape, BF),
            pltpu.SemaphoreType.DMA((7,)),
            pltpu.VMEM((rows, DN), F32),
            pltpu.VMEM((2, 256, 4 * DN), BF),
            pltpu.VMEM((2, 256, 4 * DN), BF),
            pltpu.VMEM((2, 256, 256), F32),
            pltpu.VMEM((2, rows // 2, 4 * DN), BF),
            pltpu.VMEM((2, rows // 2, 4 * DN), BF),
            pltpu.VMEM((rows, DN), F32),
        ],
        compiler_params=pltpu.CompilerParams(vmem_limit_bytes=60 << 20),
        cost_estimate=pl.CostEstimate(flops=1_500_000_000, bytes_accessed=7_000_000, transcendentals=600_000),
    )(spot, q, latents, back_one, ahead_one, back_two, ahead_two, docs, own_w, other_w)


def from_behind(value, axis, steps):
    count = lax.axis_size(axis)
    leading, last = (max(0, -steps), min(count, count - steps))
    return lax.ppermute(value, axis, [(source, source + steps) for source in range(leading, last)])


def shards(
    delta_query_rows,
    delta_key_rows,
    delta_value_rows,
    delta_write_strength,
    token_gate_scale,
    channel_decay_rate,
    sudden_loss_mask,
    document_numbers,
    delta_norm_gain,
    delta_output_cotangent,
    latent_query_rows,
    compressed_latents,
    query_to_latent_map,
    latent_to_value_map,
):
    ranks = lax.axis_size("ctx")
    place = lax.axis_index("ctx")
    seqs = delta_query_rows.shape[0]
    rows = delta_query_rows.shape[1]
    heads = delta_query_rows.shape[2]
    value_width = delta_value_rows.shape[3]
    here = place.astype(jnp.int32).reshape(1)
    docs = document_numbers.reshape(ranks, rows)
    latents = compressed_latents[0]
    flat = lambda tensor: tensor.reshape(rows * heads, tensor.shape[3])

    groups = lax.axis_size("dp")
    member = lax.axis_index("dp")
    core = member % 2
    span = heads // 2
    keep_lift = lax.dynamic_slice_in_dim(query_to_latent_map, core * span, span, 0)
    keep_lower = lax.dynamic_slice_in_dim(latent_to_value_map, core * span, span, 0)
    lift = keep_lift.reshape(span, 4, 4, DN).transpose(0, 2, 1, 3).reshape(span * 16, DN)
    lower = keep_lower.reshape(span * 16, DN)

    def shifted(value, step):
        return lax.ppermute(value, "ctx", [((i + step) % ranks, i) for i in range(ranks)])

    across = shifted(jnp.concatenate([lift, lower], axis=0), XS * ranks // (2 * XS))
    lift = jnp.concatenate([lift, across[: span * 16]], axis=0)
    lower = jnp.concatenate([lower, across[span * 16 :]], axis=0)
    tiles = latents.reshape(2, HALF, 4, DN).transpose(0, 2, 1, 3).reshape(2, 4 * HALF, DN)
    ahead_one = shifted(jnp.concatenate([lift, lower, tiles[0], tiles[1]], axis=0), 1)
    back_one = shifted(jnp.concatenate([lift, lower, tiles[0]], axis=0), -1)
    ahead_two = shifted(jnp.concatenate([lift, tiles[1]], axis=0), 2)
    back_two = shifted(jnp.concatenate([lower, tiles[0]], axis=0), -2)
    many = span * 32
    lift = jnp.stack([lift, ahead_one[:many], ahead_two[:many], back_one[:many]])
    lift = lift.reshape(XS, 2, span, 4, 4, DN).transpose(2, 3, 0, 1, 4, 5).reshape(XS * many, DN)
    lower = jnp.concatenate(
        [lower, ahead_one[many : 2 * many], back_two[:many], back_one[many : 2 * many]], axis=0
    )
    lift = jnp.stack([lift, shifted(lift, 2 * XS)])
    lower = jnp.stack([lower, shifted(lower, -2 * XS)])
    lift = jnp.stack([lift, shifted(lift, XS)])
    lower = jnp.stack([lower, shifted(lower, -XS)])
    own_w = jnp.stack([lift, lower])
    other_w = lax.ppermute(own_w, "dp", [(i, i ^ 1) for i in range(groups)])

    lmat, att, rhs, leaving, closing, carried_q = kda_pairs(
        here,
        flat(delta_query_rows),
        flat(delta_key_rows),
        flat(delta_value_rows),
        delta_write_strength[0].T,
        token_gate_scale[0].T,
        channel_decay_rate,
        sudden_loss_mask,
        docs,
    )
    xmat = kda_invert(lmat)
    offs_first, offs_second, tmap, upd = kda_leave(xmat, rhs, leaving, closing)
    near_first = from_behind(offs_first, "ctx", 1)
    near_second = from_behind(offs_second, "ctx", -1)
    local, squery = kda_local(att, upd, carried_q)
    out_first, out_second = kda_carry(
        here, tmap, offs_first, offs_second, near_first, near_second, ranks
    )
    far_first = from_behind(out_first, "ctx", 1)
    far_second = from_behind(out_second, "ctx", -1)
    normed_rows, partial_grad = kda_close(
        here,
        local,
        squery,
        out_first,
        far_first,
        far_second,
        delta_norm_gain.reshape(1, value_width),
        flat(delta_output_cotangent),
        ranks,
    )
    kda_output = normed_rows.reshape(seqs, rows, heads, value_width)
    terms = lax.all_to_all(partial_grad, "ctx", 0, 0, tiled=True)
    spread = jnp.broadcast_to(jnp.sum(terms, axis=0), (groups, value_width))
    terms = lax.all_to_all(spread, "dp", 0, 0, tiled=True)
    total_grad = jnp.sum(terms, axis=0)
    gain_grad = total_grad / math.sqrt(seqs * groups * rows * ranks * heads)

    spot = jnp.stack([place, core]).astype(jnp.int32)
    mla_rows = mla(
        spot,
        flat(latent_query_rows),
        latents,
        back_one,
        ahead_one,
        back_two,
        ahead_two,
        docs,
        own_w,
        other_w,
        XS,
    )
    mla_output = mla_rows.reshape(seqs, rows, heads, DN)
    return (kda_output, mla_output, gain_grad)


def solution(mesh):
    placed = (
        P("dp", "ctx", None, None),
        P("dp", "ctx", None, None),
        P("dp", "ctx", None, None),
        P("dp", "ctx", None),
        P("dp", "ctx", None),
        P(),
        P("dp", "ctx"),
        P("dp", None),
        P(),
        P("dp", "ctx", None, None),
        P("dp", "ctx", None, None),
        P("dp", "ctx", None),
        P(None, "ctx", None),
        P(None, "ctx", None),
    )
    return jax.shard_map(
        shards,
        mesh=mesh,
        in_specs=placed,
        out_specs=(P("dp", "ctx", None, None), P("dp", "ctx", None, None), P()),
        check_vma=False,
    )
```

```python
import functools
import math

import jax
import jax.numpy as jnp
from jax import lax
from jax.experimental import pallas as pl
from jax.experimental.pallas import tpu as pltpu
from jax.sharding import PartitionSpec as P

DN = 128
XS = 4
HALF = 64
F32 = jnp.float32
BF = jnp.bfloat16
LOSS = math.log(0.6)


def mm(a, b):
    return lax.dot_general(a, b, (((1,), (0,)), ((), ())), preferred_element_type=F32)


def mm_nt(a, b):
    return lax.dot_general(a, b, (((1,), (1,)), ((), ())), preferred_element_type=F32)


def mm_tn(a, b):
    return lax.dot_general(a, b, (((0,), (0,)), ((), ())), preferred_element_type=F32)


def iota2(shape, dim):
    return lax.broadcasted_iota(jnp.int32, shape, dim)


def docs_row(docs_ref, block):
    row = docs_ref[pl.ds(block // 2, 1), :].astype(F32)
    odd = jnp.full((1, HALF), block % 2, jnp.int32)
    return jnp.where(odd == 1, row[:, HALF:], row[:, :HALF])


def as_column(row):
    size = row.shape[1]
    eye = iota2((size, size), 0) == iota2((size, size), 1)
    return jnp.sum(jnp.where(eye, jnp.broadcast_to(row, (size, size)), 0.0), axis=1, keepdims=True)


def kda_pairs_kernel(
    place_ref, q_hbm, k_hbm, v_hbm, w_ref, scale_ref, rate_ref, mask_ref, docs_ref,
    lmat, att, rhs, leaving, closing, carried_q,
    q_ref, k_ref, v_ref, sems, qn, kn, vn, acol, wcol, bcol, ccol, tcol, incl, excl,
):
    heads = rate_ref.shape[0]
    place = place_ref[0]
    ranks = docs_ref.shape[0]
    rows = HALF * heads

    copies = [
        pltpu.make_async_copy(source, target, sems.at[n])
        for n, (source, target) in enumerate(((q_hbm, q_ref), (k_hbm, k_ref), (v_hbm, v_ref)))
    ]
    for copy in copies:
        copy.start()

    ti, si = iota2((HALF, HALF), 0), iota2((HALF, HALF), 1)
    scales = scale_ref[...].T
    strengths = w_ref[...].T
    for i in range(2):
        block = place if i == 0 else 2 * ranks - 1 - place
        drow = docs_row(docs_ref, block)
        prior = docs_row(docs_ref, jnp.maximum(block - 1, 0))[:, HALF - 1 :]
        prior = jnp.where(jnp.full((1, 1), block, jnp.int32) > 0, prior, -1.0)
        dcol = as_column(drow)
        same = dcol == drow
        within = jnp.where(same & (ti >= si), 1.0, 0.0)
        incl[i] = within
        excl[i] = jnp.where(same & (ti > si), 1.0, 0.0)
        gates = lax.dot_general(
            within, scales[i * HALF : (i + 1) * HALF, :], (((1,), (0,)), ((), ())),
            precision=lax.Precision.HIGHEST, preferred_element_type=F32,
        )
        lost = mask_ref[:, i * HALF : (i + 1) * HALF].astype(F32)
        bcol[i] = jnp.broadcast_to(jnp.sum(within * lost, axis=1, keepdims=True) * LOSS, (HALF, DN))
        ccol[i] = jnp.broadcast_to(jnp.where(dcol == prior, 1.0, 0.0), (HALF, DN))
        tcol[i] = jnp.broadcast_to(jnp.where(dcol == drow[:, HALF - 1 :], 1.0, 0.0), (HALF, DN))
        writes = strengths[i * HALF : (i + 1) * HALF, :]
        for h in range(heads):
            acol[i * heads + h] = jnp.broadcast_to(gates[:, h : h + 1], (HALF, DN))
            wcol[i * heads + h] = jnp.broadcast_to(writes[:, h : h + 1], (HALF, DN))

    for copy in copies:
        copy.wait()

    def widen(c, _):
        at = pl.ds(pl.multiple_of(c * 256, 256), 256)
        for source, target in ((q_ref, qn), (k_ref, kn)):
            x = source[at, :].astype(F32)
            target[at, :] = x * lax.rsqrt(jnp.sum(x * x, axis=1, keepdims=True) + 1e-06)
        vn[at, :] = v_ref[at, :].astype(F32)
        return 0

    lax.fori_loop(0, 2 * rows // 256, widen, 0)

    def pairs(g, _):
        for u in range(4):
            p = g * 4 + u
            i = p // heads
            h = p % heads
            at = pl.ds(i * rows + h, HALF, stride=heads)
            q, k, v = qn[at, :], kn[at, :], vn[at, :]
            w = wcol[p]
            carried = ccol[i]
            cumlog = bcol[i] - acol[p] * rate_ref[pl.ds(h, 1), :]
            grow = jnp.exp(cumlog)
            kd, qd = k * grow, q * grow
            kg = k * jnp.exp(-cumlog)
            both = jnp.concatenate([kd, qd], axis=0)
            both_hi, kg_hi = both.astype(BF), kg.astype(BF)
            both_lo = (both - both_hi.astype(F32)).astype(BF)
            kg_lo = (kg - kg_hi.astype(F32)).astype(BF)
            inner = mm_nt(both_hi, kg_hi) + mm_nt(both_hi, kg_lo) + mm_nt(both_lo, kg_hi)
            lmat[p] = inner[:HALF] * w[:, :HALF] * excl[i]
            att[p] = (inner[HALF:] * incl[i]).astype(BF)
            rhs[p, :, :DN] = (w * v).astype(BF)
            rhs[p, :, DN:] = (w * carried * kd).astype(BF)
            carried_q[p] = (carried * qd).astype(BF)
            last = grow[HALF - 1 :, :]
            leaving[p] = (kg * last * tcol[i]).astype(BF)
            closing[p] = jnp.broadcast_to(carried[HALF - 1 :, :] * last, (8, DN))
        return 0

    lax.fori_loop(0, 2 * heads // 4, pairs, 0)


def kda_pairs(place, q, k, v, w, scale, rate, mask, docs):
    heads = rate.shape[0]
    n = 2 * heads
    rows = q.shape[0]
    vm = lambda *s: pltpu.VMEM(s, F32)
    spec = pl.BlockSpec(memory_space=pltpu.VMEM)
    shapes = (
        jax.ShapeDtypeStruct((n, HALF, HALF), F32),
        jax.ShapeDtypeStruct((n, HALF, HALF), BF),
        jax.ShapeDtypeStruct((n, HALF, 2 * DN), BF),
        jax.ShapeDtypeStruct((n, HALF, DN), BF),
        jax.ShapeDtypeStruct((n, 8, DN), F32),
        jax.ShapeDtypeStruct((n, HALF, DN), BF),
    )
    return pl.pallas_call(
        kda_pairs_kernel,
        name="kda_pairs",
        out_shape=shapes,
        in_specs=[pl.BlockSpec(memory_space=pltpu.SMEM)]
        + [pl.BlockSpec(memory_space=pltpu.HBM)] * 3
        + [spec] * 5,
        out_specs=(spec,) * 6,
        scratch_shapes=[
            pltpu.VMEM((rows, DN), BF), pltpu.VMEM((rows, DN), BF), pltpu.VMEM((rows, DN), BF),
            pltpu.SemaphoreType.DMA((3,)),
            vm(rows, DN), vm(rows, DN), vm(rows, DN),
            vm(n, HALF, DN), vm(n, HALF, DN),
            vm(2, HALF, DN), vm(2, HALF, DN), vm(2, HALF, DN),
            vm(2, HALF, HALF), vm(2, HALF, HALF),
        ],
        compiler_params=pltpu.CompilerParams(vmem_limit_bytes=60 << 20),
        cost_estimate=pl.CostEstimate(flops=300_000_000, bytes_accessed=12_000_000, transcendentals=600_000),
    )(place, q, k, v, w, scale, rate, mask, docs)


def kda_invert_kernel(lmat, xmat, pick, coef):
    heads = lmat.shape[0] // 2
    ti, si = iota2((HALF, HALF), 0), iota2((HALF, HALF), 1)

    kk, lane = iota2((4 * HALF, DN), 0), iota2((4 * HALF, DN), 1)
    side = (kk // DN) == (lane // HALF)
    for j in range(15):
        pick[:, j * DN : (j + 1) * DN] = jnp.where(side & (kk % 16 == j), 1.0, 0.0).astype(BF)
    near = (ti // 16) == (si // 16)
    rowi, coli = iota2((8, DN), 0), iota2((8, DN), 1) % HALF

    def base(g, _):
        wide = []
        for u in range(4):
            parts = []
            for v in range(2):
                lower = jnp.where(near, lmat[g * 8 + 2 * u + v], 0.0)
                high = lower.astype(BF).astype(F32)
                parts += [high, lower - high]
            wide.append(jnp.concatenate(parts, axis=1).astype(BF))
        coef[...] = mm(jnp.concatenate(wide, axis=0), pick[...])
        for u in range(4):
            made = []
            for b in range(HALF // 16):
                top = jnp.where(coli == rowi + 16 * b, 1.0, 0.0)
                low = jnp.where(coli == rowi + 16 * b + 8, 1.0, 0.0)
                at = u * HALF + 16 * b
                for j in range(15):
                    lanes = slice(j * DN, (j + 1) * DN)
                    row = top[j : j + 1, :] if j < 8 else low[j - 8 : j - 7, :]
                    if j < 7:
                        top = top - coef[at : at + 8, lanes] * row
                    low = low - coef[at + 8 : at + 16, lanes] * row
                made += [top, low]
            x = jnp.concatenate(made, axis=0)
            xmat[g * 8 + 2 * u] = x[:, :HALF]
            xmat[g * 8 + 2 * u + 1] = x[:, HALF:]
        return 0

    lax.fori_loop(0, heads // 4, base, 0)

    def merge(width, g, _):
        tb, sb = ti // width, si // width
        cross = ((tb % 2) == 1) & (sb == tb - 1)
        for u in range(8):
            p = g * 8 + u
            x = xmat[p]
            xb = x.astype(BF)
            y = mm(jnp.where(cross, lmat[p], 0.0).astype(BF), xb)
            xmat[p] = x - mm(xb, y.astype(BF))
        return 0

    lax.fori_loop(0, heads // 4, functools.partial(merge, 16), 0)
    lax.fori_loop(0, heads // 4, functools.partial(merge, 32), 0)


def kda_invert(lmat):
    spec = pl.BlockSpec(memory_space=pltpu.VMEM)
    return pl.pallas_call(
        kda_invert_kernel,
        name="kda_invert",
        out_shape=jax.ShapeDtypeStruct(lmat.shape, F32),
        in_specs=[spec],
        out_specs=spec,
        scratch_shapes=[pltpu.VMEM((4 * HALF, 15 * DN), BF), pltpu.VMEM((4 * HALF, 15 * DN), F32)],
        compiler_params=pltpu.CompilerParams(vmem_limit_bytes=16 << 20),
        cost_estimate=pl.CostEstimate(flops=300_000_000, bytes_accessed=12_000_000, transcendentals=0),
    )(lmat)


def kda_leave_kernel(xmat, rhs, leaving, closing, behind, offs_first, offs_second, tmap, upd):
    heads = xmat.shape[0] // 2

    offs_first[heads * DN :, :] = behind[8 * HALF :, :]

    def solve(g, _):
        for u in range(8):
            p = g * 8 + u
            upd[p] = mm(xmat[p].astype(BF), rhs[p]).astype(BF)
        return 0

    lax.fori_loop(0, heads // 4, solve, 0)

    eye = iota2((DN, DN), 0) == iota2((DN, DN), 1)
    for i, target in ((0, offs_first), (1, offs_second)):

        def leave(g, _, i=i, target=target):
            for u in range(4):
                h = g * 4 + u
                p = i * heads + h
                made = mm_tn(leaving[p], upd[p])
                target[pl.ds(pl.multiple_of(h * DN, DN), DN), :] = made[:, :DN].astype(BF)
                keep = jnp.where(eye, jnp.broadcast_to(closing[p][:1, :], (DN, DN)), 0.0)
                tmap[p] = (keep - made[:, DN:]).astype(BF)
            return 0

        lax.fori_loop(0, heads // 4, leave, 0)


def kda_leave(xmat, rhs, leaving, closing, behind):
    n = xmat.shape[0]
    spec = pl.BlockSpec(memory_space=pltpu.VMEM)
    shapes = (
        jax.ShapeDtypeStruct((n // 2 * DN + 4 * HALF, DN), BF),
        jax.ShapeDtypeStruct((n // 2 * DN, DN), BF),
        jax.ShapeDtypeStruct((n, DN, DN), BF),
        jax.ShapeDtypeStruct((n, HALF, 2 * DN), BF),
    )
    return pl.pallas_call(
        kda_leave_kernel,
        name="kda_leave",
        out_shape=shapes,
        in_specs=[spec] * 5,
        out_specs=(spec,) * 4,
        compiler_params=pltpu.CompilerParams(vmem_limit_bytes=24 << 20),
        cost_estimate=pl.CostEstimate(flops=300_000_000, bytes_accessed=8_000_000, transcendentals=0),
    )(xmat, rhs, leaving, closing, behind)


def kda_local_kernel(att, upd, carried_q, local, squery):
    n = att.shape[0]

    def body(g, _):
        for u in range(8):
            p = g * 8 + u
            made = mm(att[p], upd[p])
            local[p] = made[:, :DN]
            squery[p] = (carried_q[p].astype(F32) - made[:, DN:]).astype(BF)
        return 0

    lax.fori_loop(0, n // 8, body, 0)


def kda_local(att, upd, carried_q):
    n = att.shape[0]
    spec = pl.BlockSpec(memory_space=pltpu.VMEM)
    return pl.pallas_call(
        kda_local_kernel,
        name="kda_local",
        out_shape=(jax.ShapeDtypeStruct((n, HALF, DN), F32), jax.ShapeDtypeStruct((n, HALF, DN), BF)),
        in_specs=[spec] * 3,
        out_specs=(spec,) * 2,
        cost_estimate=pl.CostEstimate(flops=70_000_000, bytes_accessed=4_000_000, transcendentals=0),
    )(att, upd, carried_q)


def kda_carry_kernel(place_ref, tmap, offs_first, offs_second, in_first, in_second, out_first, out_second, *, ranks):
    heads = tmap.shape[0] // 2
    end = jnp.full((DN, DN), place_ref[0], jnp.int32) == ranks - 1

    def body(g, _):
        for u in range(4):
            h = g * 4 + u
            at = pl.ds(pl.multiple_of(h * DN, DN), DN)
            own = offs_first[at, :].astype(F32)
            out_first[at, :] = (own + mm(tmap[h], in_first[at, :])).astype(BF)
            upper = jnp.where(end, own, in_second[at, :].astype(F32)).astype(BF)
            out_second[at, :] = (
                offs_second[at, :].astype(F32) + mm(tmap[heads + h], upper)
            ).astype(BF)
        return 0

    lax.fori_loop(0, heads // 4, body, 0)


def kda_carry(place, tmap, offs_first, offs_second, in_first, in_second, ranks):
    spec = pl.BlockSpec(memory_space=pltpu.VMEM)
    shape = jax.ShapeDtypeStruct(offs_second.shape, BF)
    return pl.pallas_call(
        functools.partial(kda_carry_kernel, ranks=ranks),
        name="kda_carry",
        out_shape=(shape, shape),
        in_specs=[pl.BlockSpec(memory_space=pltpu.SMEM)] + [spec] * 5,
        out_specs=(spec, spec),
        cost_estimate=pl.CostEstimate(flops=130_000_000, bytes_accessed=5_000_000, transcendentals=0),
    )(place, tmap, offs_first, offs_second, in_first, in_second)


def kda_close_kernel(place_ref, local, squery, own_first, in_first, in_second, gain, cot_hbm, out_ref, grad_ref, cot_ref, sem, cot, outs, *, ranks):
    heads = local.shape[0] // 2
    rows = HALF * heads
    end = jnp.full((DN, DN), place_ref[0], jnp.int32) == ranks - 1
    copy = pltpu.make_async_copy(cot_hbm, cot_ref, sem)
    copy.start()
    copy.wait()

    def widen(c, _):
        at = pl.ds(pl.multiple_of(c * 256, 256), 256)
        cot[at, :] = cot_ref[at, :].astype(F32)
        return 0

    lax.fori_loop(0, 2 * rows // 256, widen, 0)

    def body(g, grad):
        for u in range(4):
            h = g * 4 + u
            state_at = pl.ds(pl.multiple_of(h * DN, DN), DN)
            upper = jnp.where(
                end, own_first[state_at, :].astype(F32), in_second[state_at, :].astype(F32)
            ).astype(BF)
            for i, state in ((0, in_first[state_at, :]), (1, upper)):
                p = i * heads + h
                raw = local[p] + mm(squery[p], state)
                normed = raw * lax.rsqrt(jnp.mean(raw * raw, axis=1, keepdims=True) + 1e-06)
                at = pl.ds(i * rows + h, HALF, stride=heads)
                outs[at, :] = normed * gain[...]
                terms = normed * cot[at, :]
                grad = grad + jnp.sum(terms.reshape(HALF // 8, 8, DN), axis=0)
        return grad

    grad = lax.fori_loop(0, heads // 4, body, jnp.zeros((8, DN), F32))
    grad_ref[...] = jnp.broadcast_to(jnp.sum(grad, axis=0, keepdims=True), grad_ref.shape)

    def narrow(c, _):
        at = pl.ds(pl.multiple_of(c * 256, 256), 256)
        out_ref[at, :] = outs[at, :].astype(BF)
        return 0

    lax.fori_loop(0, 2 * rows // 256, narrow, 0)


def kda_close(place, local, squery, own_first, in_first, in_second, gain, cot, ranks):
    spec = pl.BlockSpec(memory_space=pltpu.VMEM)
    rows = cot.shape[0]
    return pl.pallas_call(
        functools.partial(kda_close_kernel, ranks=ranks),
        name="kda_close",
        out_shape=(jax.ShapeDtypeStruct((rows, DN), BF), jax.ShapeDtypeStruct((ranks, DN), F32)),
        in_specs=[pl.BlockSpec(memory_space=pltpu.SMEM)] + [spec] * 6 + [pl.BlockSpec(memory_space=pltpu.HBM)],
        out_specs=(spec, spec),
        scratch_shapes=[
            pltpu.VMEM((rows, DN), BF), pltpu.SemaphoreType.DMA,
            pltpu.VMEM((rows, DN), F32), pltpu.VMEM((rows, DN), F32)],
        compiler_params=pltpu.CompilerParams(vmem_limit_bytes=32 << 20),
        cost_estimate=pl.CostEstimate(flops=70_000_000, bytes_accessed=5_000_000, transcendentals=4096),
    )(place, local, squery, own_first, in_first, in_second, gain, cot)


def onehot(shape, source):
    return jnp.where(iota2(shape, 0) == source(iota2(shape, 1)), 1.0, 0.0).astype(BF)


def mla_lift_kernel(spot_ref, q_hbm, own_hbm, other_hbm, lifted, q_ref, own_w, other_w, sems, qp, *, xs, ranks):
    place, core = spot_ref[0], spot_ref[1]
    heads = q_ref.shape[0] // (2 * HALF)
    moves = ((q_hbm, q_ref), (own_hbm.at[0], own_w), (other_hbm.at[0], other_w))
    copies = [pltpu.make_async_copy(a, b, sems.at[n]) for n, (a, b) in enumerate(moves)]
    for copy in copies:
        copy.start()

    def source_n(k):
        turn, column = k // 64 + 2 * ((k // 32) % 2) + 4 * ((k // 4) % 2), (k // 8) % xs
        shift = jnp.where(column == xs - 1, -1, column) + xs * turn
        return ((shift + place + ranks) % ranks) * 4 + k % 4

    pick = onehot((DN, DN), source_n)
    rows = 256
    copies[0].wait()

    def place_q(c, _):
        at = pl.ds(pl.multiple_of(c * rows, rows), rows)
        qp[at, :] = mm(q_ref[at, :], pick)
        return 0

    lax.fori_loop(0, q_ref.shape[0] // rows, place_q, 0)
    span = heads // 2
    for side, weights in ((0, own_w), (1, other_w)):
        first = span * core if side == 0 else span * (1 - core)
        copies[1 + side].wait()

        def lift(g, _, weights=weights, first=first):
            for u in range(2):
                hl = g * 2 + u
                h = first + hl
                q = qp[pl.ds(h, 2 * HALF, stride=heads), :].astype(BF)
                for lb in range(4):
                    at = pl.ds(pl.multiple_of((hl * 4 + lb) * 32, 32), 32)
                    w = jnp.concatenate(
                        [weights[e, b, at, :] for e in range(2) for b in range(2)], axis=0
                    )
                    made = mm(q, w).astype(BF)
                    for i in range(2):
                        dst = pl.ds(pl.multiple_of(h * HALF, HALF), HALF)
                        lifted[i, dst, lb * DN : (lb + 1) * DN] = made[i * HALF : (i + 1) * HALF]
            return 0

        lax.fori_loop(0, span // 2, lift, 0)


def mla_lift(spot, q, own_w, other_w, xs, ranks):
    hbm = pl.BlockSpec(memory_space=pltpu.HBM)
    rows = q.shape[0]
    return pl.pallas_call(
        functools.partial(mla_lift_kernel, xs=xs, ranks=ranks),
        name="mla_lift",
        out_shape=jax.ShapeDtypeStruct((2, rows // 2, 4 * DN), BF),
        in_specs=[pl.BlockSpec(memory_space=pltpu.SMEM), hbm, hbm, hbm],
        out_specs=pl.BlockSpec(memory_space=pltpu.VMEM),
        scratch_shapes=[
            pltpu.VMEM((rows, DN), BF),
            pltpu.VMEM(own_w.shape[1:], BF),
            pltpu.VMEM(own_w.shape[1:], BF),
            pltpu.SemaphoreType.DMA((3,)),
            pltpu.VMEM((rows, DN), F32),
        ],
        compiler_params=pltpu.CompilerParams(vmem_limit_bytes=60 << 20),
        cost_estimate=pl.CostEstimate(flops=400_000_000, bytes_accessed=5_000_000, transcendentals=0),
    )(spot, q, own_w, other_w)


def mla_mix_kernel(
    spot_ref, lifted, lat_ref, back_one_hbm, ahead_one_hbm, back_two_hbm, ahead_two_hbm, docs_ref, own_hbm, other_hbm, out_ref,
    back_one, ahead_one, back_two, ahead_two, own_w, other_w, sems, keys, keysp, mask, mixed, outs, *, xs,
):
    ranks = docs_ref.shape[0]
    place, core = spot_ref[0], spot_ref[1]
    heads = out_ref.shape[0] // (2 * HALF)
    rows = 256
    quarter = pl.ds(8 * HALF, 4 * HALF)
    moves = (
        (back_two_hbm.at[pl.ds(heads * DN, 4 * HALF), :], back_two),
        (back_one_hbm.at[quarter, :], back_one),
        (ahead_two_hbm.at[quarter, :], ahead_two),
        (ahead_one_hbm.at[pl.ds(8 * HALF, 8 * HALF), :], ahead_one),
        (own_hbm.at[1], own_w),
        (other_hbm.at[1], other_w),
    )
    copies = [pltpu.make_async_copy(a, b, sems.at[n]) for n, (a, b) in enumerate(moves)]
    for copy in copies:
        copy.start()
    width = keys.shape[1]

    def piece(ref, at, i, slot):
        for lb in range(4):
            keys[i, slot * HALF : (slot + 1) * HALF, lb * DN : (lb + 1) * DN] = ref[
                at + lb * HALF : at + (lb + 1) * HALF, :
            ]

    keys[0, 3 * HALF :, :] = jnp.zeros((width - 3 * HALF, 4 * DN), BF)
    keys[1, 3 * HALF :, :] = jnp.zeros((width - 3 * HALF, 4 * DN), BF)
    for copy in copies[:4]:
        copy.wait()
    piece(back_two, 0, 0, 0)
    piece(back_one, 0, 0, 1)
    keys[0, 2 * HALF : 3 * HALF, :] = lat_ref[:HALF, :]
    keys[1, 2 * HALF : 3 * HALF, :] = lat_ref[HALF:, :]

    @pl.when(place < ranks - 2)
    def _():
        piece(ahead_two, 0, 1, 0)

    @pl.when(place == ranks - 2)
    def _():
        piece(ahead_one, 0, 1, 0)

    @pl.when(place == ranks - 1)
    def _():
        piece(back_one, 0, 1, 0)
        keys[1, HALF : 2 * HALF, :] = lat_ref[:HALF, :]

    @pl.when(place < ranks - 1)
    def _():
        piece(ahead_one, 4 * HALF, 1, 1)

    def source_l(k):
        turn, column = 7 * (k // 256) + 2 * ((k // 128) % 2) + 4 * ((k // 16) % 2), (k // 32) % xs
        shift = jnp.where(column == xs - 1, -1, column) + xs * turn
        return ((shift + place + ranks) % ranks) * 16 + k % 16

    spread = onehot((4 * DN, 4 * DN), source_l)
    ti, si = iota2((HALF, HALF), 0), iota2((HALF, HALF), 1)
    for i in range(2):
        keysp[i] = mm(keys[i], spread).astype(BF)
        block = place if i == 0 else 2 * ranks - 1 - place
        drow = docs_row(docs_ref, block)
        dcol = as_column(drow)
        for back in range(3):
            source = block - back
            krow = docs_row(docs_ref, jnp.maximum(source, 0))
            krow = jnp.where(jnp.full((1, HALF), source, jnp.int32) >= 0, krow, -1.0)
            allowed = dcol == krow
            if back == 0:
                allowed = allowed & (ti >= si)
            fill = jnp.where(allowed, 0.0, -1e30)
            for r in range(4):
                mask[i, r * HALF : (r + 1) * HALF, (2 - back) * HALF : (3 - back) * HALF] = fill
        mask[i, :, 3 * HALF :] = jnp.full((4 * HALF, width - 3 * HALF), -1e30, F32)

    scale = 1.0 / math.sqrt(DN)

    def attend(g, _):
        i = g // (heads // 4)
        at = pl.ds(pl.multiple_of((g % (heads // 4)) * rows, rows), rows)
        logits = mm_nt(lifted[i, at, :], keys[i]) * scale + mask[i]
        peak = jnp.max(logits, axis=1, keepdims=True)
        expo = jnp.exp(logits - peak)
        probs = (expo / jnp.sum(expo, axis=1, keepdims=True)).astype(BF)
        mixed[i, at, :] = mm(probs, keysp[i]).astype(BF)
        return 0

    lax.fori_loop(0, heads // 2, attend, 0)

    span = heads // 2
    for side, weights in ((0, own_w), (1, other_w)):
        first = span * core if side == 0 else span * (1 - core)

        copies[4 + side].wait()

        def lower(g, _, weights=weights, first=first):
            for u in range(2):
                hl = g * 2 + u
                h = first + hl
                w = jnp.concatenate(
                    [
                        weights[e, b, pl.ds(pl.multiple_of((c * span + hl) * 16, 16), 16), :]
                        for e in range(2) for b in range(2) for c in range(8)
                    ],
                    axis=0,
                )
                src = pl.ds(pl.multiple_of(h * HALF, HALF), HALF)
                both = jnp.concatenate([mixed[0, src, :], mixed[1, src, :]], axis=0)
                outs[pl.ds(h, 2 * HALF, stride=heads), :] = mm(both, w)
            return 0

        lax.fori_loop(0, span // 2, lower, 0)

    def narrow(c, _):
        at = pl.ds(pl.multiple_of(c * rows, rows), rows)
        out_ref[at, :] = outs[at, :].astype(BF)
        return 0

    lax.fori_loop(0, out_ref.shape[0] // rows, narrow, 0)


def mla_mix(spot, lifted, latents, back_one, ahead_one, back_two, ahead_two, docs, own_w, other_w, xs):
    spec = pl.BlockSpec(memory_space=pltpu.VMEM)
    hbm = pl.BlockSpec(memory_space=pltpu.HBM)
    rows = 2 * lifted.shape[1]
    return pl.pallas_call(
        functools.partial(mla_mix_kernel, xs=xs),
        name="mla_mix",
        out_shape=jax.ShapeDtypeStruct((rows, DN), BF),
        in_specs=[pl.BlockSpec(memory_space=pltpu.SMEM), spec, spec, hbm, hbm, hbm, hbm, spec, hbm, hbm],
        out_specs=spec,
        scratch_shapes=[
            pltpu.VMEM((4 * HALF, DN), BF),
            pltpu.VMEM((8 * HALF, DN), BF),
            pltpu.VMEM((4 * HALF, DN), BF),
            pltpu.VMEM((4 * HALF, DN), BF),
            pltpu.VMEM(own_w.shape[1:], BF),
            pltpu.VMEM(own_w.shape[1:], BF),
            pltpu.SemaphoreType.DMA((6,)),
            pltpu.VMEM((2, 256, 4 * DN), BF),
            pltpu.VMEM((2, 256, 4 * DN), BF),
            pltpu.VMEM((2, 256, 256), F32),
            pltpu.VMEM((2, rows // 2, 4 * DN), BF),
            pltpu.VMEM((rows, DN), F32),
        ],
        compiler_params=pltpu.CompilerParams(vmem_limit_bytes=60 << 20),
        cost_estimate=pl.CostEstimate(flops=1_100_000_000, bytes_accessed=6_000_000, transcendentals=600_000),
    )(spot, lifted, latents, back_one, ahead_one, back_two, ahead_two, docs, own_w, other_w)


def from_behind(value, axis, steps):
    count = lax.axis_size(axis)
    leading, last = (max(0, -steps), min(count, count - steps))
    return lax.ppermute(value, axis, [(source, source + steps) for source in range(leading, last)])


def shards(
    delta_query_rows,
    delta_key_rows,
    delta_value_rows,
    delta_write_strength,
    token_gate_scale,
    channel_decay_rate,
    sudden_loss_mask,
    document_numbers,
    delta_norm_gain,
    delta_output_cotangent,
    latent_query_rows,
    compressed_latents,
    query_to_latent_map,
    latent_to_value_map,
):
    ranks = lax.axis_size("ctx")
    place = lax.axis_index("ctx")
    seqs = delta_query_rows.shape[0]
    rows = delta_query_rows.shape[1]
    heads = delta_query_rows.shape[2]
    value_width = delta_value_rows.shape[3]
    here = place.astype(jnp.int32).reshape(1)
    docs = document_numbers.reshape(ranks, rows)
    latents = compressed_latents[0]
    flat = lambda tensor: tensor.reshape(rows * heads, tensor.shape[3])

    groups = lax.axis_size("dp")
    member = lax.axis_index("dp")
    core = member % 2
    span = heads // 2
    keep_lift = lax.dynamic_slice_in_dim(query_to_latent_map, core * span, span, 0)
    keep_lower = lax.dynamic_slice_in_dim(latent_to_value_map, core * span, span, 0)
    lift = keep_lift.reshape(span, 4, 4, DN).transpose(0, 2, 1, 3).reshape(span * 16, DN)
    lower = keep_lower.reshape(span * 16, DN)

    def shifted(value, step):
        return lax.ppermute(value, "ctx", [((i + step) % ranks, i) for i in range(ranks)])

    across = shifted(jnp.concatenate([lift, lower], axis=0), XS * ranks // (2 * XS))
    lift = jnp.concatenate([lift, across[: span * 16]], axis=0)
    lower = jnp.concatenate([lower, across[span * 16 :]], axis=0)
    tiles = latents.reshape(2, HALF, 4, DN).transpose(0, 2, 1, 3).reshape(2, 4 * HALF, DN)
    ahead_one = shifted(jnp.concatenate([lift, lower, tiles[0], tiles[1]], axis=0), 1)
    back_one = shifted(jnp.concatenate([lift, lower, tiles[0]], axis=0), -1)
    ahead_two = shifted(jnp.concatenate([lift, lower, tiles[1]], axis=0), 2)
    many = span * 32
    lift = jnp.stack([lift, ahead_one[:many], ahead_two[:many], back_one[:many]])
    lift = lift.reshape(XS, 2, span, 4, 4, DN).transpose(2, 3, 0, 1, 4, 5).reshape(XS * many, DN)
    lower = jnp.concatenate(
        [lower, ahead_one[many : 2 * many], ahead_two[many : 2 * many], back_one[many : 2 * many]], axis=0
    )
    both = jnp.stack([lift, lower])
    moved = shifted(both, 2 * XS)
    lift = jnp.stack([both[0], moved[0]])
    lower = jnp.stack([both[1], moved[1]])
    lift = jnp.stack([lift, shifted(lift, XS)])
    lower = jnp.stack([lower, shifted(lower, -XS)])
    own_w = jnp.stack([lift, lower])
    other_w = lax.ppermute(own_w, "dp", [(i, i ^ 1) for i in range(groups)])

    lmat, att, rhs, leaving, closing, carried_q = kda_pairs(
        here,
        flat(delta_query_rows),
        flat(delta_key_rows),
        flat(delta_value_rows),
        delta_write_strength[0].T,
        token_gate_scale[0].T,
        channel_decay_rate,
        sudden_loss_mask,
        docs,
    )
    xmat = kda_invert(lmat)
    offs_first, offs_second, tmap, upd = kda_leave(xmat, rhs, leaving, closing, back_one)
    near_first = from_behind(offs_first, "ctx", 1)
    near_second = from_behind(offs_second, "ctx", -1)
    local, squery = kda_local(att, upd, carried_q)
    out_first, out_second = kda_carry(
        here, tmap, offs_first, offs_second, near_first, near_second, ranks
    )
    far_first = from_behind(out_first, "ctx", 1)
    far_second = from_behind(out_second, "ctx", -1)
    normed_rows, partial_grad = kda_close(
        here,
        local,
        squery,
        out_first,
        far_first,
        far_second,
        delta_norm_gain.reshape(1, value_width),
        flat(delta_output_cotangent),
        ranks,
    )
    kda_output = normed_rows.reshape(seqs, rows, heads, value_width)
    terms = lax.all_to_all(partial_grad, "ctx", 0, 0, tiled=True)
    spread = jnp.broadcast_to(jnp.sum(terms, axis=0), (groups, value_width))
    terms = lax.all_to_all(spread, "dp", 0, 0, tiled=True)
    total_grad = jnp.sum(terms, axis=0)
    gain_grad = total_grad / math.sqrt(seqs * groups * rows * ranks * heads)

    spot = jnp.stack([place, core]).astype(jnp.int32)
    lifted = mla_lift(spot, flat(latent_query_rows), own_w, other_w, XS, ranks)
    mla_rows = mla_mix(
        spot, lifted, latents, back_one, ahead_one, near_first, ahead_two, docs, own_w, other_w, XS
    )
    mla_output = mla_rows.reshape(seqs, rows, heads, DN)
    return (kda_output, mla_output, gain_grad)


def solution(mesh):
    placed = (
        P("dp", "ctx", None, None),
        P("dp", "ctx", None, None),
        P("dp", "ctx", None, None),
        P("dp", "ctx", None),
        P("dp", "ctx", None),
        P(),
        P("dp", "ctx"),
        P("dp", None),
        P(),
        P("dp", "ctx", None, None),
        P("dp", "ctx", None, None),
        P("dp", "ctx", None),
        P(None, "ctx", None),
        P(None, "ctx", None),
    )
    return jax.shard_map(
        shards,
        mesh=mesh,
        in_specs=placed,
        out_specs=(P("dp", "ctx", None, None), P("dp", "ctx", None, None), P()),
        check_vma=False,
    )
```
